256 devices in a mesh: row: 32 (over y, x, z_hi), col: 8 (over z_lo, core).
Axes of the slice: x: 4, y: 4, z: 8 (z_hi: 2, z_lo: 4; z = z_hi * 4 + z_lo), core: 2. Of those that a mesh axis runs over, the one named last changes fastest.
Arguments:
- alignment: bfloat16 [64, 1536, 256], P('row', 'col'), may hold values from -6 to 6
- pair_act: bfloat16 [1536, 1536, 128], P('row', 'col'), may hold values from -600 to 600
- targets: int32 [1536, 1536], P('row', 'col'), may hold values from 0 to 63, as said below
- crop_mask: int32 [1536], replicated, may hold values 0 or 1
- projection_weight: bfloat16 [256, 64], replicated, may hold values from -0.375 to 0.375
- w_outer: bfloat16 [1024, 128], replicated, may hold values from -1.5 to 1.5
- w_expand: bfloat16 [128, 512], replicated, may hold values from -0.5 to 0.5
- w_shrink: bfloat16 [512, 128], replicated, may hold values from -0.25 to 0.25
- w_bins: bfloat16 [128, 64], replicated, may hold values from -1.8 to 1.8
Outputs:
- pair_grad: bfloat16 [1536, 1536, 128], P('row', 'col')
The draws below stay inside these ranges and needn't reach their ends.
Inputs may be any that keep to these rules, and one draw needn't show every extreme that they name: targets[i, j] equals targets[j, i].
All inputs are finite; a program needn't handle non-finite values.
Results may differ from the reference program's by a relative error of at most 0.02.
The reference program's roundings to bfloat16 on the way count: a program that leaves them out, or rounds other values in their place, can miss the bound.
Values may be sent and summed in bfloat16 or wider, within the bound.
A program may use at most 128 MiB of HBM per device.

```python
import jax
import jax.numpy as jnp
from jax import lax

ALIGNMENT_CHANS = 256
PAIR_CH = 128
FACTOR_CHANNELS = 32
HIDDEN_CH = 512
BINS = 64
SEQUENCE_COUNT = 64
CROP_RESIDUES = 1536


def draw_pair_act(key, part):
    key_base = jax.random.fold_in(key, 0)
    base = jnp.clip(jax.random.normal(key_base, (CROP_RESIDUES, CROP_RESIDUES, PAIR_CH), jnp.float32), -6.0, 6.0)
    return base.astype(jnp.bfloat16)


def draw_targets(key, part):
    drawn = jax.random.randint(key, (CROP_RESIDUES, CROP_RESIDUES), 0, BINS, dtype=jnp.int32)
    upper = jnp.arange(CROP_RESIDUES)[:, None] <= jnp.arange(CROP_RESIDUES)[None, :]
    return jnp.where(upper, drawn, drawn.T)


def draw_w_bins(key, part):
    key_base = jax.random.fold_in(key, 0)
    base = jnp.clip(0.3 * jax.random.normal(key_base, (PAIR_CH, BINS), jnp.float32), -1.8, 1.8)
    return base.astype(jnp.bfloat16)


def plant(result, rng, smallest, high):
    longest = result.shape.index(max(result.shape))
    spots = []
    for shift in (0, 1):
        where = [jax.random.randint(jax.random.fold_in(rng, axis), (), 0, length) for axis, length in enumerate(result.shape)]
        where[longest] = (where[longest] + shift) % result.shape[longest]
        spots.append(tuple(where))
    return result.at[spots[0]].set(smallest).at[spots[1]].set(high)


def level_of(own_key, shape, cuts, least, largest):
    factor_of = 1.0
    for axis_at, parts in cuts:
        draws = jax.random.uniform(jax.random.fold_in(jax.random.fold_in(own_key, 6), axis_at), (parts,), jnp.float32, least / len(cuts), largest / len(cuts))
        factor_of = factor_of * jnp.repeat(jnp.exp(draws), shape[axis_at] // parts).reshape((-1,) + (1,) * (len(shape) - 1 - axis_at))
    return factor_of


def normal_values(rng, dims, spread, bound, cuts=(), held_as=jnp.bfloat16):
    values = jax.random.normal(rng, dims, jnp.float32) * spread
    if len(cuts) > 0:
        values = level_of(rng, dims, cuts, -0.22, 0.18) * values
    return jnp.clip(values, min=-bound, max=bound).astype(held_as)


def setup_inputs(seed: int = 0) -> dict:
    streams_of = jax.random.split(jax.random.key(seed), 10)
    alignment = normal_values(streams_of[0], (SEQUENCE_COUNT, CROP_RESIDUES, ALIGNMENT_CHANS), 1.0, 6.0, ((0, 32), (1, 8)))
    pair_act = draw_pair_act(jax.random.fold_in(streams_of[9], 71), 0)
    targets = draw_targets(jax.random.fold_in(streams_of[9], 71), 0)
    crop_mask = plant((jax.random.randint(streams_of[3], (CROP_RESIDUES,), 0, 8) < 7).astype(jnp.int32), jax.random.fold_in(streams_of[3], 1), 0, 1)
    projection_weight = normal_values(streams_of[4], (ALIGNMENT_CHANS, 2 * FACTOR_CHANNELS), ALIGNMENT_CHANS ** -0.5, 0.375)
    w_outer = normal_values(streams_of[5], (FACTOR_CHANNELS * FACTOR_CHANNELS, PAIR_CH), (FACTOR_CHANNELS * FACTOR_CHANNELS // SEQUENCE_COUNT) ** -0.5, 1.5)
    w_expand = normal_values(streams_of[6], (PAIR_CH, HIDDEN_CH), PAIR_CH ** -0.5, 0.5)
    w_shrink = normal_values(streams_of[7], (HIDDEN_CH, PAIR_CH), HIDDEN_CH ** -0.5, 0.25)
    w_bins = draw_w_bins(jax.random.fold_in(streams_of[9], 71), 0)
    return dict(alignment=alignment, pair_act=pair_act, targets=targets, crop_mask=crop_mask, projection_weight=projection_weight, w_outer=w_outer, w_expand=w_expand, w_shrink=w_shrink, w_bins=w_bins)


epsilon = 1e-05

def layer_normalize(values):
    average = lax.optimization_barrier(jnp.mean(values, axis=-1, keepdims=True))
    centred = values - average
    inverse_deviation = lax.rsqrt(lax.optimization_barrier(jnp.mean(centred * centred, axis=-1, keepdims=True)) + epsilon)
    return (centred * inverse_deviation, inverse_deviation)

def reference(alignment, pair_act, targets, crop_mask, projection_weight, w_outer, w_expand, w_shrink, w_bins):
    normed = layer_normalize(alignment.astype(jnp.float32))[0].astype(jnp.bfloat16)
    factors = jnp.dot(normed, projection_weight, preferred_element_type=jnp.float32).astype(jnp.bfloat16)
    left_side = factors[:, :, :FACTOR_CHANNELS].astype(jnp.float32)
    right_side = factors[:, :, FACTOR_CHANNELS:].astype(jnp.float32)
    block_rows = 16
    blocks = CROP_RESIDUES // block_rows
    mask_float = crop_mask.astype(jnp.float32)

    def transition(middle_state):
        xnorm = layer_normalize(middle_state.astype(jnp.float32))[0].astype(jnp.bfloat16)
        before = lax.optimization_barrier(jnp.dot(xnorm, w_expand, preferred_element_type=jnp.float32).astype(jnp.bfloat16))
        hidden = jax.nn.silu(before.astype(jnp.float32)).astype(jnp.bfloat16)
        final = (middle_state.astype(jnp.float32) + jnp.dot(hidden, w_shrink, preferred_element_type=jnp.float32)).astype(jnp.bfloat16)
        return (before, final)

    def forward(block_index):
        first_row = block_index * block_rows
        left_rows = lax.dynamic_slice_in_dim(left_side, first_row, block_rows, 1)
        outer = jnp.einsum('sic,sje->ijce', left_rows, right_side) / SEQUENCE_COUNT
        outer = outer.reshape(block_rows * CROP_RESIDUES, FACTOR_CHANNELS * FACTOR_CHANNELS).astype(jnp.bfloat16)
        update = jnp.dot(outer, w_outer, preferred_element_type=jnp.float32)
        pair_rows = lax.dynamic_slice_in_dim(pair_act, first_row, block_rows, 0).reshape(block_rows * CROP_RESIDUES, PAIR_CH)
        middle_state = (pair_rows.astype(jnp.float32) + update).astype(jnp.bfloat16)
        before, final = transition(middle_state)
        logits = jnp.dot(final, w_bins, preferred_element_type=jnp.float32).astype(jnp.bfloat16)
        return (middle_state, logits.reshape(block_rows, CROP_RESIDUES, BINS))
    middles, logits = lax.map(forward, jnp.arange(blocks, dtype=jnp.int32))
    logits = logits.reshape(CROP_RESIDUES, CROP_RESIDUES, BINS)

    def backward(block_index):
        first_row = block_index * block_rows
        middle_state = middles[block_index]
        own = lax.dynamic_slice_in_dim(logits, first_row, block_rows, 0)
        across = lax.dynamic_slice_in_dim(logits, first_row, block_rows, 1).transpose(1, 0, 2)
        scores = own.astype(jnp.float32) + across.astype(jnp.float32)
        scores = scores - lax.optimization_barrier(jnp.max(scores, axis=-1, keepdims=True))
        expo = jnp.exp(scores)
        prob = expo / lax.optimization_barrier(jnp.sum(expo, axis=-1, keepdims=True))
        target_rows = lax.dynamic_slice_in_dim(targets, first_row, block_rows, 0)
        onehot = (target_rows[:, :, None] == jnp.arange(BINS, dtype=jnp.int32)).astype(jnp.float32)
        row_mask = lax.dynamic_slice_in_dim(mask_float, first_row, block_rows, 0)
        weight = row_mask[:, None] * mask_float[None, :]
        dlogits = (2.0 * (prob - onehot) * weight[:, :, None]).astype(jnp.bfloat16)
        dlogits = dlogits.reshape(block_rows * CROP_RESIDUES, BINS)
        final_gradient = jnp.dot(dlogits, w_bins.T, preferred_element_type=jnp.float32)
        before, final = transition(middle_state)
        before_f = before.astype(jnp.float32)
        sigma = jax.nn.sigmoid(before_f)
        slope = sigma * (1.0 + before_f * (1.0 - sigma))
        dhidden = (jnp.dot(final_gradient.astype(jnp.bfloat16), w_shrink.T, preferred_element_type=jnp.float32) * slope).astype(jnp.bfloat16)
        normed_input_gradient = jnp.dot(dhidden, w_expand.T, preferred_element_type=jnp.float32)
        standardized_input, inverse_deviation = layer_normalize(middle_state.astype(jnp.float32))
        middle_gradient = final_gradient + inverse_deviation * (normed_input_gradient - lax.optimization_barrier(jnp.mean(normed_input_gradient, axis=-1, keepdims=True)) - standardized_input * lax.optimization_barrier(jnp.mean(normed_input_gradient * standardized_input, axis=-1, keepdims=True)))
        return middle_gradient.astype(jnp.bfloat16).reshape(block_rows, CROP_RESIDUES, PAIR_CH)
    grads = lax.map(backward, jnp.arange(blocks, dtype=jnp.int32))
    return grads.reshape(CROP_RESIDUES, CROP_RESIDUES, PAIR_CH)
```

```python
import functools

import jax
import jax.numpy as jnp
from jax import lax
from jax.experimental import pallas as pl
from jax.experimental.pallas import tpu as pltpu
from jax.sharding import PartitionSpec as P

MESH = pl.DeviceIdType.MESH
F32 = jnp.float32
BF16 = jnp.bfloat16
EPS = 1e-05
ROWS, COLS, CH = 48, 192, 128
HALF = 24
HID = 512


def dot(a, b):
    return lax.dot_general(a, b, (((1,), (0,)), ((), ())), preferred_element_type=F32)


def normalize(x):
    mean = jnp.mean(x, axis=-1, keepdims=True)
    centred = x - mean
    scale = lax.rsqrt(jnp.mean(centred * centred, axis=-1, keepdims=True) + EPS)
    return centred * scale, scale


def kernel(
    al, pair, t2, pw_right, place, w_outer_t, w_expand, w_shrink, bins2, shrink_t, expand_t, bins2_t,
    out,
    g_right, g_left, own_left, f_right, f_left, left_op, outer_op, middle, slope, logits, arrived, mirror,
    right_send, right_recv, left_send, left_recv, mir_send, mir_recv,
):
    r = lax.axis_index("row")
    c = lax.axis_index("col")
    z = lax.rem(r, 2)
    partner = r + 1 - 2 * z
    root = r // 4
    quarter = lax.rem(r, 4)

    bar = pltpu.get_barrier_semaphore()
    pl.semaphore_signal(bar, inc=1, device_id=(partner, c), device_id_type=MESH)

    def greet_plane(k, _):
        m = lax.rem(r // 2 + k, 16)
        pl.semaphore_signal(bar, inc=1, device_id=(2 * m + z, c), device_id_type=MESH)
        return 0

    lax.fori_loop(1, 16, greet_plane, 0)

    def greet_left(k, _):
        @pl.when(jnp.logical_or(k != r, root != c))
        def _():
            pl.semaphore_signal(bar, inc=1, device_id=(k, root), device_id_type=MESH)

        return 0

    lax.fori_loop(0, 32, greet_left, 0)
    for a in range(4):
        @pl.when(jnp.logical_or(4 * c + a != r, root != c))
        def _():
            pl.semaphore_signal(bar, inc=1, device_id=(4 * c + a, root), device_id_type=MESH)

    normed = []
    for s in range(2):
        normed.append(normalize(al[s].astype(F32))[0])
    tails = []
    for s in range(2):
        ft = lax.dot_general(
            pw_right[...], normed[s].astype(BF16), (((1,), (1,)), ((), ())), preferred_element_type=F32
        )
        g_right[r, pl.ds(32 * s, 32), :] = ft[:, :128].astype(BF16)
        tails.append(ft[:, 128:192])
    g_right[r, pl.ds(64, 32), :] = jnp.concatenate(tails, axis=1).astype(BF16)
    lf = None
    for h in range(2):
        for s in range(2):
            rows = jnp.concatenate(
                [normed[s][q * ROWS + h * HALF : q * ROWS + h * HALF + HALF] for q in range(4)], axis=0
            ).astype(BF16)
            term = dot(rows, place[2 * h + s])
            lf = term if lf is None else lf + term
    for q in range(4):
        own_left[q] = jnp.concatenate(
            [lf[q * HALF : (q + 1) * HALF], jnp.zeros((8, 128), F32)], axis=0
        ).astype(BF16)

    is_root = (root == c).astype(jnp.int32)
    pl.semaphore_wait(bar, 52 - 2 * is_root)

    def right_copy(block, slot, dest):
        return pltpu.make_async_remote_copy(
            src_ref=g_right.at[block], dst_ref=g_right.at[block],
            send_sem=right_send.at[slot], recv_sem=right_recv.at[block],
            device_id=(dest, c), device_id_type=MESH,
        )

    right_copy(r, 0, partner).start()

    def start_own(k, _):
        m = lax.rem(r // 2 + k, 16)
        right_copy(r, k, 2 * m + z).start()
        return 0

    lax.fori_loop(1, 16, start_own, 0)

    def left_copy(k):
        return pltpu.make_async_remote_copy(
            src_ref=own_left.at[k // 8], dst_ref=g_left.at[r],
            send_sem=left_send.at[k], recv_sem=left_recv.at[r],
            device_id=(4 * c + k // 8, lax.rem(k, 8)), device_id_type=MESH,
        )

    def left_self(k):
        return jnp.logical_and(4 * c + k // 8 == r, lax.rem(k, 8) == c)

    def start_left(k, _):
        mine = left_self(k)

        @pl.when(mine)
        def _():
            pltpu.make_async_copy(own_left.at[k // 8], g_left.at[r], left_recv.at[r]).start()

        @pl.when(jnp.logical_not(mine))
        def _():
            left_copy(k).start()

        return 0

    lax.fori_loop(0, 32, start_left, 0)

    right_copy(partner, 0, partner).wait_recv()

    def start_partner(k, _):
        m = lax.rem(r // 2 + k, 16)
        right_copy(partner, 15 + k, 2 * m + z).start()
        return 0

    lax.fori_loop(1, 16, start_partner, 0)

    def wait_left(k, _):
        pltpu.make_async_copy(g_left.at[k], g_left.at[k], left_recv.at[k]).wait()
        return 0

    lax.fori_loop(0, 32, wait_left, 0)

    def left_rows(k, _):
        f_left[pl.ds(pl.multiple_of(k * 32, 32), 32), :] = g_left[k].astype(F32) * (1.0 / 64.0)
        return 0

    lax.fori_loop(0, 32, left_rows, 0)

    def left_block(p, _):
        x = f_left[pl.ds(p, 32, stride=32), :]
        stack = jnp.concatenate([x] + [pltpu.roll(x, 128 - 32 * g, axis=1) for g in range(1, 4)], axis=0)
        left_op[pl.ds(pl.multiple_of(p * 32, 32), 32), :] = stack.T[:32].astype(BF16)
        return 0

    lax.fori_loop(0, HALF, left_block, 0)

    def wait_right(k, _):
        m = lax.rem(r // 2 + k, 16)
        right_copy(2 * m + z, 0, partner).wait_recv()
        right_copy(2 * m + 1 - z, 0, partner).wait_recv()
        return 0

    lax.fori_loop(1, 16, wait_right, 0)

    def right_rows(k, _):
        f_right[pl.ds(pl.multiple_of(k * 96, 96), 96), :] = g_right[k].astype(F32)
        return 0

    lax.fori_loop(0, 32, right_rows, 0)

    low = lax.broadcasted_iota(jnp.int32, (32, 128), 1) < 64

    def outer_step(e2, _):
        ab, tail = [], []
        zero = jnp.zeros((32, 128), F32)
        for par in range(2):
            e = 2 * e2 + par
            x0 = f_right[pl.ds(e, 32, stride=96), :]
            x1 = f_right[pl.ds(e + 32, 32, stride=96), :]
            xb = f_right[pl.ds(e + 64, 32, stride=96), :]
            xr = pltpu.roll(xb, 64, axis=1)
            h0 = jnp.concatenate([x0, x1, zero, zero], axis=0)
            h1 = jnp.concatenate([zero, zero, x0, x1], axis=0)
            ab.append(jnp.concatenate([h0, h1], axis=1).astype(BF16))
            tail.append(
                jnp.concatenate(
                    [
                        jnp.where(low, xb, zero), jnp.where(low, xr, zero),
                        jnp.where(low, zero, xr), jnp.where(low, zero, xb),
                    ],
                    axis=0,
                ).astype(BF16)
            )
        chunks = ab + [jnp.concatenate(tail, axis=1)]
        for which in range(3):
            for mb in range(6):
                res = dot(left_op[mb * 128 : (mb + 1) * 128, :], chunks[which]).astype(BF16)
                for pi in range(4):
                    p = mb * 4 + pi
                    piece = res[pi * 32 : (pi + 1) * 32]
                    if which < 2:
                        rows = pl.ds(pl.multiple_of((2 * e2 + which) * 32, 32), 32)
                        outer_op[p // 2, rows, pl.ds((p % 2) * 384, 256)] = piece
                    else:
                        for par in range(2):
                            rows = pl.ds(pl.multiple_of((2 * e2 + par) * 32, 32), 32)
                            outer_op[p // 2, rows, pl.ds((p % 2) * 384 + 256, 128)] = piece[
                                :, par * 128 : (par + 1) * 128
                            ]
        return 0

    lax.fori_loop(0, 16, outer_step, 0)

    def mirror_copy(st, a):
        return pltpu.make_async_remote_copy(
            src_ref=logits.at[pl.ds(2 * st, 2), pl.ds(a * ROWS, ROWS), :],
            dst_ref=arrived.at[quarter, pl.ds(2 * st, 2), :, :],
            send_sem=mir_send.at[st, a], recv_sem=mir_recv.at[st, quarter],
            device_id=(4 * c + a, root), device_id_type=MESH,
        )

    def mirror_is_self(a):
        return jnp.logical_and(4 * c + a == r, root == c)

    def forward_step(st, _):
        upd_t = dot(w_outer_t[...], outer_op[st])
        upd = [upd_t[:, k * 128 : (k + 1) * 128].T for k in range(6)]
        for t in range(2):
            p = 2 * st + t
            finals = []
            for h in range(2):
                i = p + HALF * h
                update = jnp.concatenate(
                    [upd[3 * t + h], upd[3 * t + 2][h * 64 : (h + 1) * 64]], axis=0
                )
                mid = (pair[i].astype(F32) + update).astype(BF16)
                middle[i] = mid
                mid = mid.astype(F32)
                xn = normalize(mid)[0].astype(BF16)
                before = dot(xn, w_expand[...]).astype(BF16).astype(F32)
                sig = 0.5 * jnp.tanh(0.5 * before) + 0.5
                hid = before * sig
                slope[i] = (sig + hid * (1.0 - sig)).astype(BF16)
                finals.append((mid + dot(hid.astype(BF16), w_shrink[...])).astype(BF16))
            logits[p] = dot(jnp.concatenate(finals, axis=1), bins2[...]).astype(BF16)
        for a in range(4):
            mine = mirror_is_self(a)

            @pl.when(mine)
            def _():
                pltpu.make_async_copy(
                    logits.at[pl.ds(2 * st, 2), pl.ds(a * ROWS, ROWS), :],
                    arrived.at[quarter, pl.ds(2 * st, 2), :, :],
                    mir_recv.at[st, quarter],
                ).start()

            @pl.when(jnp.logical_not(mine))
            def _():
                mirror_copy(st, a).start()

        return 0

    lax.fori_loop(0, 12, forward_step, 0)

    def take_mirror(st, _):
        for s in range(4):
            pltpu.make_async_copy(
                arrived.at[s, pl.ds(2 * st, 2), :, :], arrived.at[s, pl.ds(2 * st, 2), :, :], mir_recv.at[st, s]
            ).wait()
            for t in range(2):
                q = 2 * st + t
                rows = pl.ds(pl.multiple_of(s * 1152 + q * ROWS, 16), ROWS)
                mirror[rows, :] = arrived[s, q].astype(F32)
        return 0

    lax.fori_loop(0, 12, take_mirror, 0)

    lane = lax.broadcasted_iota(jnp.int32, (COLS, 128), 1)
    first = lane < 64
    code = lax.rem(lane, 64).astype(F32)
    sel_row = lax.broadcasted_iota(jnp.int32, (128, 128), 0)
    sel_half = HALF * (lax.broadcasted_iota(jnp.int32, (128, 128), 1) // 64)
    small = lax.broadcasted_iota(jnp.int32, (HALF, 128), 1) < 64

    def backward_step(p, _):
        parts = []
        for s in range(4):
            x0 = mirror[pl.ds(s * 1152 + p, HALF, stride=ROWS), :]
            x1 = mirror[pl.ds(s * 1152 + p + HALF, HALF, stride=ROWS), :]
            parts.append(jnp.where(small, x0, pltpu.roll(x1, 64, axis=1)))
            parts.append(jnp.where(small, pltpu.roll(x0, 64, axis=1), x1))
        scores = logits[p].astype(F32) + jnp.concatenate(parts, axis=0)
        low_max = jnp.max(jnp.where(first, scores, -jnp.inf), axis=-1, keepdims=True)
        high_max = jnp.max(jnp.where(first, -jnp.inf, scores), axis=-1, keepdims=True)
        expo = jnp.exp(scores - jnp.where(first, low_max, high_max))
        low_sum = jnp.sum(jnp.where(first, expo, 0.0), axis=-1, keepdims=True)
        high_sum = jnp.sum(jnp.where(first, 0.0, expo), axis=-1, keepdims=True)
        prob = expo * jnp.where(first, 1.0 / low_sum, 1.0 / high_sum)
        pick_t = (sel_row == sel_half + p).astype(BF16)
        pick_w = (sel_row == sel_half + (p + 64)).astype(BF16)
        goal = dot(t2[...], pick_t)
        weight = dot(t2[...], pick_w)
        dlog = ((prob - jnp.where(goal == code, 1.0, 0.0)) * weight).astype(BF16)
        dfin = dot(dlog, bins2_t[...])
        for h in range(2):
            i = p + HALF * h
            grad = dfin[:, h * 128 : (h + 1) * 128]
            dh = (dot(grad.astype(BF16), shrink_t[...]) * slope[i].astype(F32)).astype(BF16)
            dxn = dot(dh, expand_t[...])
            xhat, scale = normalize(middle[i].astype(F32))
            g1 = jnp.mean(dxn, axis=-1, keepdims=True)
            g2 = jnp.mean(dxn * xhat, axis=-1, keepdims=True)
            out[i] = (grad + scale * (dxn - g1 - xhat * g2)).astype(BF16)
        return 0

    lax.fori_loop(0, HALF, backward_step, 0)

    def drain_right(k, _):
        right_copy(r, k, partner).wait_send()
        return 0

    lax.fori_loop(0, 31, drain_right, 0)

    def drain_left(k, _):
        @pl.when(jnp.logical_not(left_self(k)))
        def _():
            left_copy(k).wait_send()

        return 0

    lax.fori_loop(0, 32, drain_left, 0)

    def drain_mirror(st, _):
        for a in range(4):
            @pl.when(jnp.logical_not(mirror_is_self(a)))
            def _():
                mirror_copy(st, a).wait_send()

        return 0

    lax.fori_loop(0, 12, drain_mirror, 0)


def per_device(
    alignment, pair_act, targets, crop_mask, projection_weight, w_outer, w_expand, w_shrink, w_bins
):
    row = lax.axis_index("row")
    col = lax.axis_index("col")
    row_mask = lax.dynamic_slice_in_dim(crop_mask, row * ROWS, ROWS)
    col_mask = lax.dynamic_slice_in_dim(crop_mask, col * COLS, COLS)
    weight = 2 * col_mask[:, None] * row_mask[None, :]
    pad = jnp.zeros((COLS, 16), jnp.int32)
    t2 = jnp.concatenate([targets.T, pad, weight, pad], axis=1).astype(BF16)
    pw_right = projection_weight[:, 32:].T
    left_w = projection_weight[:, :32]
    place = jnp.stack([jnp.pad(left_w, ((0, 0), (32 * g, 96 - 32 * g))) for g in range(4)])
    w_outer_t = w_outer.reshape(32, 32, CH).transpose(2, 1, 0).reshape(CH, 1024)
    zero = jnp.zeros_like(w_bins)
    bins2 = jnp.concatenate(
        [jnp.concatenate([w_bins, zero], axis=1), jnp.concatenate([zero, w_bins], axis=1)], axis=0
    )
    vmem = pl.BlockSpec(memory_space=pltpu.VMEM)
    return pl.pallas_call(
        kernel,
        out_shape=jax.ShapeDtypeStruct((ROWS, COLS, CH), BF16),
        in_specs=[vmem] * 12,
        out_specs=vmem,
        scratch_shapes=[
            pltpu.VMEM((32, 96, 128), BF16),
            pltpu.VMEM((32, 32, 128), BF16),
            pltpu.VMEM((4, 32, 128), BF16),
            pltpu.VMEM((3072, 128), F32),
            pltpu.VMEM((1024, 128), F32),
            pltpu.VMEM((768, 128), BF16),
            pltpu.VMEM((12, 1024, 768), BF16),
            pltpu.VMEM((ROWS, COLS, CH), BF16),
            pltpu.VMEM((ROWS, COLS, HID), BF16),
            pltpu.VMEM((HALF, COLS, 128), BF16),
            pltpu.VMEM((4, HALF, ROWS, 128), BF16),
            pltpu.VMEM((4 * HALF * ROWS, 128), F32),
            pltpu.SemaphoreType.DMA((31,)),
            pltpu.SemaphoreType.DMA((32,)),
            pltpu.SemaphoreType.DMA((32,)),
            pltpu.SemaphoreType.DMA((32,)),
            pltpu.SemaphoreType.DMA((12, 4)),
            pltpu.SemaphoreType.DMA((12, 4)),
        ],
        compiler_params=pltpu.CompilerParams(
            collective_id=0, has_side_effects=True, vmem_limit_bytes=63 * 1024 * 1024
        ),
    )(
        alignment, pair_act, t2, pw_right, place, w_outer_t, w_expand, w_shrink, bins2,
        w_shrink.T, w_expand.T, bins2.T,
    )


def solution(mesh):
    in_specs = (
        P("row", "col", None), P("row", "col", None), P("row", "col"),
        P(), P(), P(), P(), P(), P(),
    )
    return jax.shard_map(
        per_device, mesh=mesh, in_specs=in_specs, out_specs=P("row", "col", None), check_vma=False
    )
```

```python
import functools

import jax
import jax.numpy as jnp
from jax import lax
from jax.experimental import pallas as pl
from jax.experimental.pallas import tpu as pltpu
from jax.sharding import PartitionSpec as P

MESH = pl.DeviceIdType.MESH
F32 = jnp.float32
BF16 = jnp.bfloat16
EPS = 1e-05
ROWS, COLS, CH = 48, 192, 128
HALF = 24
HID = 512
OUTER_BLOCKS = 1
BACK_ROWS = 2
FORWARD_GROUP = 4


def dot(a, b):
    return lax.dot_general(a, b, (((1,), (0,)), ((), ())), preferred_element_type=F32)


def normalize(x):
    mean = jnp.mean(x, axis=-1, keepdims=True)
    centred = x - mean
    scale = lax.rsqrt(jnp.mean(centred * centred, axis=-1, keepdims=True) + EPS)
    return centred * scale, scale


def kernel(
    al, pair, targets, mask_rows, mask, pw, w_outer, w_expand, w_shrink, w_bins,
    out,
    g_right, g_left, own_left, f_right, f_left, left_op, outer_op, middle, slope, logits, arrived, mirror,
    relay, w_outer_t, half_expand, bins2, half_shrink_t, expand_t, bins2_t, goals,
    right_send, right_recv, left_send, left_recv, mir_send, mir_recv, relay_send, relay_recv, pass_send,
):
    r = lax.axis_index("row")
    c = lax.axis_index("col")
    z = lax.rem(r, 2)
    partner = r + 1 - 2 * z
    root = r // 4
    quarter = lax.rem(r, 4)
    y = r // 8
    diagonal = y == c // 2
    off_diagonal = jnp.logical_not(diagonal)
    in_plane = lax.rem(r, 8)

    bar = pltpu.get_barrier_semaphore()
    pl.semaphore_signal(bar, inc=1, device_id=(partner, c), device_id_type=MESH)

    def greet_plane(k, _):
        m = lax.rem(r // 2 + k, 16)
        pl.semaphore_signal(bar, inc=1, device_id=(2 * m + z, c), device_id_type=MESH)
        return 0

    lax.fori_loop(1, 16, greet_plane, 0)

    def greet_left(k, _):
        @pl.when(jnp.logical_or(k != r, root != c))
        def _():
            pl.semaphore_signal(bar, inc=1, device_id=(k, root), device_id_type=MESH)

        return 0

    lax.fori_loop(0, 32, greet_left, 0)
    for a in range(4):
        @pl.when(jnp.logical_or(4 * c + a != r, root != c))
        def _():
            pl.semaphore_signal(bar, inc=1, device_id=(4 * c + a, root), device_id_type=MESH)

    @pl.when(off_diagonal)
    def _():
        for s in range(4):
            pl.semaphore_signal(
                bar, inc=1, device_id=(8 * y + lax.rem(4 * c + s, 8), root), device_id_type=MESH
            )

    @pl.when(diagonal)
    def _():
        for k in range(1, 4):
            pl.semaphore_signal(
                bar, inc=1, device_id=(8 * lax.rem(y + k, 4) + in_plane, c), device_id_type=MESH
            )

    pw_pad = jnp.concatenate([pw[...].astype(F32), jnp.zeros((256, 64), F32)], axis=1)
    pw_right = pw_pad.T[32:64].astype(BF16)
    pw_left = jnp.where(lax.broadcasted_iota(jnp.int32, (256, 128), 1) < 32, pw_pad, 0.0)

    normed = []
    for s in range(2):
        normed.append(normalize(al[s].astype(F32))[0])
    tails = []
    for s in range(2):
        ft = lax.dot_general(
            pw_right, normed[s].astype(BF16), (((1,), (1,)), ((), ())), preferred_element_type=F32
        )
        g_right[r, pl.ds(32 * s, 32), :] = ft[:, :128].astype(BF16)
        tails.append(ft[:, 128:192])
    g_right[r, pl.ds(64, 32), :] = jnp.concatenate(tails, axis=1).astype(BF16)
    lf = None
    for h in range(2):
        for s in range(2):
            rows = jnp.concatenate(
                [normed[s][q * ROWS + h * HALF : q * ROWS + h * HALF + HALF] for q in range(4)], axis=0
            ).astype(BF16)
            shift = 32 * (2 * h + s)
            place = pltpu.roll(pw_left, shift, axis=1) if shift else pw_left
            term = dot(rows, place.astype(BF16))
            lf = term if lf is None else lf + term
    for q in range(4):
        own_left[q] = jnp.concatenate(
            [lf[q * HALF : (q + 1) * HALF], jnp.zeros((8, 128), F32)], axis=0
        ).astype(BF16)

    is_root = (root == c).astype(jnp.int32)
    on_diagonal = diagonal.astype(jnp.int32)
    pl.semaphore_wait(bar, 53 - 2 * is_root + 11 * on_diagonal)

    def right_copy(block, slot, dest):
        return pltpu.make_async_remote_copy(
            src_ref=g_right.at[block], dst_ref=g_right.at[block],
            send_sem=right_send.at[slot], recv_sem=right_recv.at[block],
            device_id=(dest, c), device_id_type=MESH,
        )

    right_copy(r, 0, partner).start()

    def start_own(k, _):
        m = lax.rem(r // 2 + k, 16)
        right_copy(r, k, 2 * m + z).start()
        return 0

    lax.fori_loop(1, 16, start_own, 0)

    def left_copy(k):
        return pltpu.make_async_remote_copy(
            src_ref=own_left.at[k // 8], dst_ref=g_left.at[r],
            send_sem=left_send.at[k], recv_sem=left_recv.at[r],
            device_id=(4 * c + k // 8, lax.rem(k, 8)), device_id_type=MESH,
        )

    def left_self(k):
        return jnp.logical_and(4 * c + k // 8 == r, lax.rem(k, 8) == c)

    def start_left(k, _):
        mine = left_self(k)

        @pl.when(mine)
        def _():
            pltpu.make_async_copy(own_left.at[k // 8], g_left.at[r], left_recv.at[r]).start()

        @pl.when(jnp.logical_not(mine))
        def _():
            left_copy(k).start()

        return 0

    lax.fori_loop(0, 32, start_left, 0)

    for k in range(4):
        cols = slice(k * 128, (k + 1) * 128)
        half_shrink_t[:, cols] = (0.5 * w_shrink[cols, :].astype(F32)).T.astype(BF16)
        expand_t[cols, :] = w_expand[:, cols].astype(F32).T.astype(BF16)
    half_expand[...] = (0.5 * w_expand[...].astype(F32)).astype(BF16)
    wb = jnp.concatenate([w_bins[...].astype(F32), jnp.zeros((128, 64), F32)], axis=1)
    wb_high = pltpu.roll(wb, 64, axis=1)
    bins2[0:128, :] = wb.astype(BF16)
    bins2[128:256, :] = wb_high.astype(BF16)
    bins2_t[:, 0:128] = wb.T.astype(BF16)
    bins2_t[:, 128:256] = wb_high.T.astype(BF16)
    mirror[0:1024, :] = w_outer[...].astype(F32)
    for k in range(8):
        block = jnp.concatenate([mirror[pl.ds(4 * k + e, 32, stride=32), :] for e in range(4)], axis=0)
        w_outer_t[:, k * 128 : (k + 1) * 128] = block.T.astype(BF16)
    table = jnp.concatenate(
        [
            targets[...].astype(F32),
            2.0 * mask_rows[pl.ds(c, 1), :].astype(F32),
            jnp.zeros((79, COLS), F32),
        ],
        axis=0,
    )
    table = jnp.concatenate([table, jnp.zeros((128, 64), F32)], axis=1)
    goals[...] = jnp.concatenate([table[:, :128].T, table[:, 128:].T[:64]], axis=0).astype(BF16)

    right_copy(partner, 0, partner).wait_recv()

    def start_partner(k, _):
        m = lax.rem(r // 2 + k, 16)
        right_copy(partner, 15 + k, 2 * m + z).start()
        return 0

    lax.fori_loop(1, 16, start_partner, 0)

    def wait_left(k, _):
        pltpu.make_async_copy(g_left.at[k], g_left.at[k], left_recv.at[k]).wait()
        return 0

    lax.fori_loop(0, 32, wait_left, 0)

    def left_rows(k, _):
        f_left[pl.ds(pl.multiple_of(k * 32, 32), 32), :] = g_left[k].astype(F32) * (1.0 / 64.0)
        return 0

    lax.fori_loop(0, 32, left_rows, 0)

    def left_block(p, _):
        x = f_left[pl.ds(p, 32, stride=32), :]
        stack = jnp.concatenate([x] + [pltpu.roll(x, 128 - 32 * g, axis=1) for g in range(1, 4)], axis=0)
        left_op[pl.ds(pl.multiple_of(p * 32, 32), 32), :] = stack.T[:32].astype(BF16)
        return 0

    lax.fori_loop(0, HALF, left_block, 0)

    def wait_right(k, _):
        m = lax.rem(r // 2 + k, 16)
        right_copy(2 * m + z, 0, partner).wait_recv()
        right_copy(2 * m + 1 - z, 0, partner).wait_recv()
        return 0

    lax.fori_loop(1, 16, wait_right, 0)

    def right_rows(k, _):
        f_right[pl.ds(pl.multiple_of(k * 96, 96), 96), :] = g_right[k].astype(F32)
        return 0

    lax.fori_loop(0, 32, right_rows, 0)

    low = lax.broadcasted_iota(jnp.int32, (32, 128), 1) < 64

    def outer_step(e2, _):
        ab, tail = [], []
        zero = jnp.zeros((32, 128), F32)
        for par in range(2):
            e = 2 * e2 + par
            x0 = f_right[pl.ds(e, 32, stride=96), :]
            x1 = f_right[pl.ds(e + 32, 32, stride=96), :]
            xb = f_right[pl.ds(e + 64, 32, stride=96), :]
            xr = pltpu.roll(xb, 64, axis=1)
            h0 = jnp.concatenate([x0, x1, zero, zero], axis=0)
            h1 = jnp.concatenate([zero, zero, x0, x1], axis=0)
            ab.append(jnp.concatenate([h0, h1], axis=1).astype(BF16))
            tail.append(
                jnp.concatenate(
                    [
                        jnp.where(low, xb, zero), jnp.where(low, xr, zero),
                        jnp.where(low, zero, xr), jnp.where(low, zero, xb),
                    ],
                    axis=0,
                ).astype(BF16)
            )
        chunks = ab + [jnp.concatenate(tail, axis=1)]
        for which in range(3):
            for mb in range(OUTER_BLOCKS):
                span = 768 // OUTER_BLOCKS
                res = dot(left_op[mb * span : (mb + 1) * span, :], chunks[which]).astype(BF16)
                for pi in range(span // 32):
                    p = mb * (span // 32) + pi
                    piece = res[pi * 32 : (pi + 1) * 32]
                    if which < 2:
                        rows = pl.ds(pl.multiple_of((2 * e2 + which) * 32, 32), 32)
                        outer_op[p // 2, rows, pl.ds((p % 2) * 384, 256)] = piece
                    else:
                        for par in range(2):
                            rows = pl.ds(pl.multiple_of((2 * e2 + par) * 32, 32), 32)
                            outer_op[p // 2, rows, pl.ds((p % 2) * 384 + 256, 128)] = piece[
                                :, par * 128 : (par + 1) * 128
                            ]
        return 0

    lax.fori_loop(0, 16, outer_step, 0)

    def mirror_copy(st, a):
        return pltpu.make_async_remote_copy(
            src_ref=logits.at[pl.ds(2 * st, 2), pl.ds(a * ROWS, ROWS), :],
            dst_ref=arrived.at[quarter, pl.ds(2 * st, 2), :, :],
            send_sem=mir_send.at[st, a], recv_sem=mir_recv.at[st, quarter],
            device_id=(4 * c + a, root), device_id_type=MESH,
        )

    def mirror_is_self(a):
        return jnp.logical_and(4 * c + a == r, root == c)

    def relay_copy(b):
        return pltpu.make_async_remote_copy(
            src_ref=logits.at[pl.ds(4 * b, 2), :, :], dst_ref=relay.at[y, b],
            send_sem=relay_send.at[b], recv_sem=relay_recv.at[y, b],
            device_id=(8 * (c // 2) + in_plane, c), device_id_type=MESH,
        )

    def pass_copy(source, b, a):
        return pltpu.make_async_remote_copy(
            src_ref=relay.at[source, b, :, pl.ds(a * ROWS, ROWS), :],
            dst_ref=arrived.at[quarter, pl.ds(4 * b, 2), :, :],
            send_sem=pass_send.at[source, b, a], recv_sem=mir_recv.at[2 * b, quarter],
            device_id=(4 * c + a, 2 * source + in_plane // 4), device_id_type=MESH,
        )

    def is_relayed(st):
        return jnp.logical_and(jnp.logical_and(off_diagonal, lax.rem(st, 2) == 0), st < 10)

    def forward_step(st, _):
        upd_t = dot(w_outer_t[...], outer_op[st])
        upd = [upd_t[:, k * 128 : (k + 1) * 128].T for k in range(6)]
        order = [(t, h) for t in range(2) for h in range(2)]
        finals = []
        for g in range(0, 4, FORWARD_GROUP):
            group = order[g : g + FORWARD_GROUP]
            ids = [2 * st + t + HALF * h for t, h in group]
            update = jnp.concatenate(
                [x for t, h in group for x in (upd[3 * t + h], upd[3 * t + 2][h * 64 : (h + 1) * 64])], axis=0
            )
            mid = (jnp.concatenate([pair[i] for i in ids], axis=0).astype(F32) + update).astype(BF16)
            for n, i in enumerate(ids):
                middle[i] = mid[n * COLS : (n + 1) * COLS]
            mid = mid.astype(F32)
            xn = normalize(mid)[0].astype(BF16)
            half = dot(xn, half_expand[...]).astype(BF16).astype(F32)
            th = jnp.tanh(half)
            hid = half + half * th
            slopes = ((1.0 + th) + (hid - hid * th)).astype(BF16)
            for n, i in enumerate(ids):
                slope[i] = slopes[n * COLS : (n + 1) * COLS]
            final = (mid + dot(hid.astype(BF16), w_shrink[...])).astype(BF16)
            finals += [final[n * COLS : (n + 1) * COLS] for n in range(FORWARD_GROUP)]
        wide = jnp.concatenate(
            [jnp.concatenate(finals[0:2], axis=1), jnp.concatenate(finals[2:4], axis=1)], axis=0
        )
        logit = dot(wide, bins2[...]).astype(BF16)
        for t in range(2):
            logits[2 * st + t] = logit[t * COLS : (t + 1) * COLS]

        @pl.when(is_relayed(st))
        def _():
            relay_copy(st // 2).start()

        @pl.when(jnp.logical_not(is_relayed(st)))
        def _():
            for a in range(4):
                mine = mirror_is_self(a)

                @pl.when(mine)
                def _():
                    pltpu.make_async_copy(
                        logits.at[pl.ds(2 * st, 2), pl.ds(a * ROWS, ROWS), :],
                        arrived.at[quarter, pl.ds(2 * st, 2), :, :],
                        mir_recv.at[st, quarter],
                    ).start()

                @pl.when(jnp.logical_not(mine))
                def _():
                    mirror_copy(st, a).start()

        @pl.when(jnp.logical_and(diagonal, jnp.logical_and(lax.rem(st, 2) == 1, st > 1)))
        def _():
            b = (st - 3) // 2
            for k in range(1, 4):
                source = lax.rem(y + k, 4)
                pltpu.make_async_copy(relay.at[source, b], relay.at[source, b], relay_recv.at[source, b]).wait()
                for a in range(4):
                    pass_copy(source, b, a).start()

        return 0

    lax.fori_loop(0, 12, forward_step, 0)

    def take_mirror(st, _):
        for s in range(4):
            pltpu.make_async_copy(
                arrived.at[s, pl.ds(2 * st, 2), :, :], arrived.at[s, pl.ds(2 * st, 2), :, :], mir_recv.at[st, s]
            ).wait()
            for t in range(2):
                q = 2 * st + t
                rows = pl.ds(pl.multiple_of(s * 1152 + q * ROWS, 16), ROWS)
                mirror[rows, :] = arrived[s, q].astype(F32)
        return 0

    lax.fori_loop(0, 12, take_mirror, 0)

    lane = lax.broadcasted_iota(jnp.int32, (COLS, 128), 1)
    first = lane < 64
    code = lax.rem(lane, 64).astype(F32)
    sel_row = lax.broadcasted_iota(jnp.int32, (128, 128), 0)
    sel_half = HALF * (lax.broadcasted_iota(jnp.int32, (128, 128), 1) // 64)
    small = lax.broadcasted_iota(jnp.int32, (HALF, 128), 1) < 64

    col_weight = jnp.broadcast_to(goals[:, 48:49].astype(F32), (COLS, 128))

    def backward_row(p):
        parts = []
        for s in range(4):
            x0 = mirror[pl.ds(s * 1152 + p, HALF, stride=ROWS), :]
            x1 = mirror[pl.ds(s * 1152 + p + HALF, HALF, stride=ROWS), :]
            parts.append(jnp.where(small, x0, pltpu.roll(x1, 64, axis=1)))
            parts.append(jnp.where(small, pltpu.roll(x0, 64, axis=1), x1))
        scores = logits[p].astype(F32) + jnp.concatenate(parts, axis=0)
        low_max = jnp.max(jnp.where(first, scores, -jnp.inf), axis=-1, keepdims=True)
        high_max = jnp.max(jnp.where(first, -jnp.inf, scores), axis=-1, keepdims=True)
        expo = jnp.exp(scores - jnp.where(first, low_max, high_max))
        low_sum = jnp.sum(jnp.where(first, expo, 0.0), axis=-1, keepdims=True)
        high_sum = jnp.sum(jnp.where(first, 0.0, expo), axis=-1, keepdims=True)
        prob = expo * jnp.where(first, 1.0 / low_sum, 1.0 / high_sum)
        goal = dot(goals[...], (sel_row == sel_half + p).astype(BF16))
        m0 = mask[r * ROWS + p].astype(F32)
        m1 = mask[r * ROWS + p + HALF].astype(F32)
        weight = col_weight * jnp.where(first, m0, m1)
        dlog = ((prob - jnp.where(goal == code, 1.0, 0.0)) * weight).astype(BF16)
        dfin = dot(dlog, bins2_t[...])
        grad = jnp.concatenate([dfin[:, :128], dfin[:, 128:]], axis=0)
        slopes = jnp.concatenate([slope[p], slope[p + HALF]], axis=0)
        dh = (dot(grad.astype(BF16), half_shrink_t[...]) * slopes.astype(F32)).astype(BF16)
        dxn = dot(dh, expand_t[...])
        mid = jnp.concatenate([middle[p], middle[p + HALF]], axis=0)
        xhat, scale = normalize(mid.astype(F32))
        g1 = jnp.mean(dxn, axis=-1, keepdims=True)
        g2 = jnp.mean(dxn * xhat, axis=-1, keepdims=True)
        res = (grad + scale * (dxn - g1 - xhat * g2)).astype(BF16)
        out[p] = res[:COLS]
        out[p + HALF] = res[COLS:]

    def backward_step(k, _):
        for t in range(BACK_ROWS):
            backward_row(BACK_ROWS * k + t)
        return 0

    lax.fori_loop(0, HALF // BACK_ROWS, backward_step, 0)

    def drain_right(k, _):
        right_copy(r, k, partner).wait_send()
        return 0

    lax.fori_loop(0, 31, drain_right, 0)

    def drain_left(k, _):
        @pl.when(jnp.logical_not(left_self(k)))
        def _():
            left_copy(k).wait_send()

        return 0

    lax.fori_loop(0, 32, drain_left, 0)

    def drain_mirror(st, _):
        @pl.when(is_relayed(st))
        def _():
            relay_copy(st // 2).wait_send()

        @pl.when(jnp.logical_not(is_relayed(st)))
        def _():
            for a in range(4):
                @pl.when(jnp.logical_not(mirror_is_self(a)))
                def _():
                    mirror_copy(st, a).wait_send()

        return 0

    lax.fori_loop(0, 12, drain_mirror, 0)

    @pl.when(diagonal)
    def _():
        def drain_pass(b, _):
            for k in range(1, 4):
                for a in range(4):
                    pass_copy(lax.rem(y + k, 4), b, a).wait_send()
            return 0

        lax.fori_loop(0, 5, drain_pass, 0)


def per_device(
    alignment, pair_act, targets, crop_mask, projection_weight, w_outer, w_expand, w_shrink, w_bins
):
    vmem = pl.BlockSpec(memory_space=pltpu.VMEM)
    return pl.pallas_call(
        kernel,
        out_shape=jax.ShapeDtypeStruct((ROWS, COLS, CH), BF16),
        in_specs=[vmem] * 4 + [pl.BlockSpec(memory_space=pltpu.SMEM)] + [vmem] * 5,
        out_specs=vmem,
        scratch_shapes=[
            pltpu.VMEM((32, 96, 128), BF16),
            pltpu.VMEM((32, 32, 128), BF16),
            pltpu.VMEM((4, 32, 128), BF16),
            pltpu.VMEM((3072, 128), F32),
            pltpu.VMEM((1024, 128), F32),
            pltpu.VMEM((768, 128), BF16),
            pltpu.VMEM((12, 1024, 768), BF16),
            pltpu.VMEM((ROWS, COLS, CH), BF16),
            pltpu.VMEM((ROWS, COLS, HID), BF16),
            pltpu.VMEM((HALF, COLS, 128), BF16),
            pltpu.VMEM((4, HALF, ROWS, 128), BF16),
            pltpu.VMEM((4 * HALF * ROWS, 128), F32),
            pltpu.VMEM((4, 5, 2, COLS, 128), BF16),
            pltpu.VMEM((128, 1024), BF16),
            pltpu.VMEM((128, HID), BF16),
            pltpu.VMEM((256, 128), BF16),
            pltpu.VMEM((128, HID), BF16),
            pltpu.VMEM((HID, 128), BF16),
            pltpu.VMEM((128, 256), BF16),
            pltpu.VMEM((COLS, 128), BF16),
            pltpu.SemaphoreType.DMA((31,)),
            pltpu.SemaphoreType.DMA((32,)),
            pltpu.SemaphoreType.DMA((32,)),
            pltpu.SemaphoreType.DMA((32,)),
            pltpu.SemaphoreType.DMA((12, 4)),
            pltpu.SemaphoreType.DMA((12, 4)),
            pltpu.SemaphoreType.DMA((5,)),
            pltpu.SemaphoreType.DMA((4, 5)),
            pltpu.SemaphoreType.DMA((4, 5, 4)),
        ],
        compiler_params=pltpu.CompilerParams(
            collective_id=0, has_side_effects=True, vmem_limit_bytes=63 * 1024 * 1024
        ),
    )(
        alignment, pair_act, targets, crop_mask.reshape(8, COLS), crop_mask, projection_weight,
        w_outer, w_expand, w_shrink, w_bins,
    )


def solution(mesh):
    in_specs = (
        P("row", "col", None), P("row", "col", None), P("row", "col"),
        P(), P(), P(), P(), P(), P(),
    )
    return jax.shard_map(
        per_device, mesh=mesh, in_specs=in_specs, out_specs=P("row", "col", None), check_vma=False
    )
```

```python
import functools

import jax
import jax.numpy as jnp
from jax import lax
from jax.experimental import pallas as pl
from jax.experimental.pallas import tpu as pltpu
from jax.sharding import PartitionSpec as P

MESH = pl.DeviceIdType.MESH
F32 = jnp.float32
BF16 = jnp.bfloat16
EPS = 1e-05
ROWS, COLS, CH = 48, 192, 128
HALF = 24
HID = 512
OUTER_BLOCKS = 1
FORWARD_GROUP = 4
BACK_ROWS = 8
CHUNK = 64
EMIT_ROWS = 12
RELAYED = 6
LAG = 2
OUTER_UNROLL = 2
BACK_UNROLL = 1
ORDER = [a * 6 + h * 3 + k for k in range(3) for a in range(4) for h in range(2)]
BACK_ORDER = [ORDER.index(n) for n in range(24)]


def dot(a, b):
    return lax.dot_general(a, b, (((1,), (0,)), ((), ())), preferred_element_type=F32)


def permute(x, order):
    return jnp.concatenate([x[8 * n : 8 * n + 8] for n in order], axis=0)


def normalize(x):
    mean = jnp.mean(x, axis=-1, keepdims=True)
    centred = x - mean
    scale = lax.rsqrt(jnp.mean(centred * centred, axis=-1, keepdims=True) + EPS)
    return centred * scale, scale


def kernel(
    al, pair, targets, mask_rows, mask, pw_t, w_outer, w_expand, w_shrink, w_bins_t,
    out,
    g_right, g_left, own_left, f_right, f_left, left_op, right_op, outer_op, middle, slope, logits, arrived, mirror,
    relay, w_outer_t, half_expand, bins2, half_shrink_t, expand_t, bins2_t, goals, upd_even, upd_odd,
    right_send, right_recv, left_send, left_recv, mir_send, mir_recv, relay_send, relay_recv, pass_send,
):
    r = lax.axis_index("row")
    c = lax.axis_index("col")
    z = lax.rem(r, 2)
    partner = r + 1 - 2 * z
    root = r // 4
    quarter = lax.rem(r, 4)
    y = r // 8
    diagonal = y == c // 2
    off_diagonal = jnp.logical_not(diagonal)
    in_plane = lax.rem(r, 8)

    bar = pltpu.get_barrier_semaphore()
    pl.semaphore_signal(bar, inc=1, device_id=(partner, c), device_id_type=MESH)

    def greet_plane(k, _):
        m = lax.rem(r // 2 + k, 16)
        pl.semaphore_signal(bar, inc=1, device_id=(2 * m + z, c), device_id_type=MESH)
        return 0

    lax.fori_loop(1, 16, greet_plane, 0)

    def greet_left(k, _):
        @pl.when(jnp.logical_or(k != r, root != c))
        def _():
            pl.semaphore_signal(bar, inc=1, device_id=(k, root), device_id_type=MESH)

        return 0

    lax.fori_loop(0, 32, greet_left, 0)
    for a in range(4):
        @pl.when(jnp.logical_or(4 * c + a != r, root != c))
        def _():
            pl.semaphore_signal(bar, inc=1, device_id=(4 * c + a, root), device_id_type=MESH)

    @pl.when(off_diagonal)
    def _():
        for s in range(4):
            pl.semaphore_signal(
                bar, inc=1, device_id=(8 * y + lax.rem(4 * c + s, 8), root), device_id_type=MESH
            )

    @pl.when(diagonal)
    def _():
        for k in range(1, 4):
            pl.semaphore_signal(
                bar, inc=1, device_id=(8 * lax.rem(y + k, 4) + in_plane, c), device_id_type=MESH
            )

    pw_right = pw_t[32:64, :]
    pw_left = pw_t[0:32, :].astype(F32)

    normed = []
    for s in range(2):
        normed.append(normalize(al[s].astype(F32))[0])
    tails = []
    for s in range(2):
        ft = lax.dot_general(
            pw_right, normed[s].astype(BF16), (((1,), (1,)), ((), ())), preferred_element_type=F32
        )
        g_right[r, pl.ds(32 * s, 32), :] = ft[:, :128].astype(BF16)
        tails.append(ft[:, 128:192])
    g_right[r, pl.ds(64, 32), :] = jnp.concatenate(tails, axis=1).astype(BF16)
    lf = None
    for h in range(2):
        for s in range(2):
            rows = jnp.concatenate(
                [normed[s][q * ROWS + h * HALF : q * ROWS + h * HALF + HALF] for q in range(4)], axis=0
            ).astype(BF16)
            before = 32 * (2 * h + s)
            place = [jnp.zeros((n, 256), F32) for n in (before, 96 - before) if n]
            place.insert(1 if before else 0, pw_left)
            place = jnp.concatenate(place, axis=0).astype(BF16)
            term = lax.dot_general(rows, place, (((1,), (1,)), ((), ())), preferred_element_type=F32)
            lf = term if lf is None else lf + term
    for q in range(4):
        own_left[q] = jnp.concatenate(
            [lf[q * HALF : (q + 1) * HALF], jnp.zeros((8, 128), F32)], axis=0
        ).astype(BF16)

    is_root = (root == c).astype(jnp.int32)
    on_diagonal = diagonal.astype(jnp.int32)
    pl.semaphore_wait(bar, 53 - 2 * is_root + 11 * on_diagonal)

    def right_copy(block, slot, dest):
        return pltpu.make_async_remote_copy(
            src_ref=g_right.at[block], dst_ref=g_right.at[block],
            send_sem=right_send.at[slot], recv_sem=right_recv.at[block],
            device_id=(dest, c), device_id_type=MESH,
        )

    right_copy(r, 0, partner).start()

    def start_own(k, _):
        m = lax.rem(r // 2 + k, 16)
        right_copy(r, k, 2 * m + z).start()
        return 0

    lax.fori_loop(1, 16, start_own, 0)

    def left_copy(k):
        return pltpu.make_async_remote_copy(
            src_ref=own_left.at[k // 8], dst_ref=g_left.at[r],
            send_sem=left_send.at[k], recv_sem=left_recv.at[r],
            device_id=(4 * c + k // 8, lax.rem(k, 8)), device_id_type=MESH,
        )

    def left_self(k):
        return jnp.logical_and(4 * c + k // 8 == r, lax.rem(k, 8) == c)

    def start_left(k, _):
        mine = left_self(k)

        @pl.when(mine)
        def _():
            pltpu.make_async_copy(own_left.at[k // 8], g_left.at[r], left_recv.at[r]).start()

        @pl.when(jnp.logical_not(mine))
        def _():
            left_copy(k).start()

        return 0

    lax.fori_loop(0, 32, start_left, 0)

    for k in range(4):
        cols = slice(k * 128, (k + 1) * 128)
        half_shrink_t[:, cols] = (0.5 * w_shrink[cols, :].astype(F32)).T.astype(BF16)
        wide = w_expand[:, cols].astype(F32)
        expand_t[cols, :] = (wide - jnp.mean(wide, axis=0, keepdims=True)).T.astype(BF16)
    half_expand[...] = (0.5 * w_expand[...].astype(F32)).astype(BF16)
    wb = jnp.concatenate([w_bins_t[...].astype(F32), jnp.zeros((64, 128), F32)], axis=0)
    wb_high = jnp.concatenate([jnp.zeros((64, 128), F32), w_bins_t[...].astype(F32)], axis=0)
    bins2[0:128, :] = wb.T.astype(BF16)
    bins2[128:256, :] = wb_high.T.astype(BF16)
    bins2_t[:, 0:128] = wb.astype(BF16)
    bins2_t[:, 128:256] = wb_high.astype(BF16)
    mirror[0:1024, :] = w_outer[...].astype(F32)
    for k in range(8):
        block = jnp.concatenate([mirror[pl.ds(4 * k + e, 32, stride=32), :] for e in range(4)], axis=0)
        w_outer_t[:, k * 128 : (k + 1) * 128] = block.T.astype(BF16)
    aims = targets[...].astype(F32)
    aims = [aims[:, :128], jnp.concatenate([aims[:, 128:], jnp.zeros((ROWS, 64), F32)], axis=1)]
    mask_a = mask_rows[pl.ds(3 * c // 2, 1), :].astype(F32)
    mask_b = mask_rows[pl.ds(3 * c // 2 + 1, 1), :].astype(F32)
    swap_a, swap_b = pltpu.roll(mask_a, 64, axis=1), pltpu.roll(mask_b, 64, axis=1)
    odd = jnp.broadcast_to(lax.rem(c, 2), (1, 128)) == 1
    low_lane = lax.broadcasted_iota(jnp.int32, (1, 128), 1) < 64
    masks = [
        jnp.where(odd, jnp.where(low_lane, swap_a, swap_b), mask_a),
        jnp.where(odd, swap_b, mask_b),
    ]
    table = [
        jnp.concatenate([x, 2.0 * m, jnp.zeros((79, 128), F32)], axis=0).T for x, m in zip(aims, masks)
    ]
    goals[...] = permute(
        jnp.concatenate([table[0], table[1][:64]], axis=0), ORDER
    ).astype(BF16).reshape(3, CHUNK, 128)

    right_copy(partner, 0, partner).wait_recv()

    def start_partner(k, _):
        m = lax.rem(r // 2 + k, 16)
        right_copy(partner, 15 + k, 2 * m + z).start()
        return 0

    lax.fori_loop(1, 16, start_partner, 0)

    def wait_left(k, _):
        pltpu.make_async_copy(g_left.at[k], g_left.at[k], left_recv.at[k]).wait()
        return 0

    lax.fori_loop(0, 32, wait_left, 0)

    def left_rows(k, _):
        f_left[pl.ds(pl.multiple_of(k * 32, 32), 32), :] = g_left[k].astype(F32) * (1.0 / 64.0)
        return 0

    lax.fori_loop(0, 32, left_rows, 0)

    def left_block(p, _):
        x = f_left[pl.ds(p, 32, stride=32), :]
        stack = jnp.concatenate([x] + [pltpu.roll(x, 128 - 32 * g, axis=1) for g in range(1, 4)], axis=0)
        left_op[pl.ds(pl.multiple_of(p * 32, 32), 32), :] = stack.T[:32].astype(BF16)
        return 0

    lax.fori_loop(0, HALF, left_block, 0)

    def wait_right(k, _):
        m = lax.rem(r // 2 + k, 16)
        right_copy(2 * m + z, 0, partner).wait_recv()
        right_copy(2 * m + 1 - z, 0, partner).wait_recv()
        return 0

    lax.fori_loop(1, 16, wait_right, 0)

    def right_rows(k, _):
        f_right[pl.ds(pl.multiple_of(k * 96, 96), 96), :] = g_right[k].astype(F32)
        return 0

    lax.fori_loop(0, 32, right_rows, 0)

    low = lax.broadcasted_iota(jnp.int32, (32, 128), 1) < 64

    def right_step(e2, _):
        ab, tail = [], []
        zero = jnp.zeros((32, 128), F32)
        for par in range(2):
            e = 2 * e2 + par
            x0 = f_right[pl.ds(e, 32, stride=96), :]
            x1 = f_right[pl.ds(e + 32, 32, stride=96), :]
            xb = f_right[pl.ds(e + 64, 32, stride=96), :]
            xr = pltpu.roll(xb, 64, axis=1)
            h0 = jnp.concatenate([x0, x1, zero, zero], axis=0)
            h1 = jnp.concatenate([zero, zero, x0, x1], axis=0)
            ab.append(jnp.concatenate([h0, h1], axis=1).astype(BF16))
            tail.append(
                jnp.concatenate(
                    [
                        jnp.where(low, xb, zero), jnp.where(low, xr, zero),
                        jnp.where(low, zero, xr), jnp.where(low, zero, xb),
                    ],
                    axis=0,
                ).astype(BF16)
            )
        for n, chunk in enumerate(ab + [jnp.concatenate(tail, axis=1)]):
            right_op[e2, n] = chunk
        return 0

    lax.fori_loop(0, 16, right_step, 0)

    def outer_block(mb):
        def outer_step(e2, _):
            lhs = left_op[pl.ds(pl.multiple_of(mb * 256, 256), 256), :]
            for which in range(3):
                res = dot(lhs, right_op[e2, which]).astype(BF16)
                for pi in range(8):
                    pp = 4 * mb + pi // 2
                    piece = res[pi * 32 : (pi + 1) * 32]
                    if which < 2:
                        rows = pl.ds(pl.multiple_of((2 * e2 + which) * 32, 32), 32)
                        outer_op[pp, rows, pl.ds((pi % 2) * 384, 256)] = piece
                    else:
                        for par in range(2):
                            rows = pl.ds(pl.multiple_of((2 * e2 + par) * 32, 32), 32)
                            outer_op[pp, rows, pl.ds((pi % 2) * 384 + 256, 128)] = piece[
                                :, par * 128 : (par + 1) * 128
                            ]
            return 0

        lax.fori_loop(0, 16, outer_step, 0, unroll=OUTER_UNROLL)

    def mirror_copy(st, a):
        return pltpu.make_async_remote_copy(
            src_ref=logits.at[st, a],
            dst_ref=arrived.at[quarter, pl.ds(2 * st, 2)],
            send_sem=mir_send.at[st, a], recv_sem=mir_recv.at[st, quarter],
            device_id=(4 * c + a, root), device_id_type=MESH,
        )

    def mirror_is_self(a):
        return jnp.logical_and(4 * c + a == r, root == c)

    def relay_copy(st):
        return pltpu.make_async_remote_copy(
            src_ref=logits.at[st], dst_ref=relay.at[y, st],
            send_sem=relay_send.at[st], recv_sem=relay_recv.at[y, st],
            device_id=(8 * (c // 2) + in_plane, c), device_id_type=MESH,
        )

    def pass_copy(source, st, a):
        return pltpu.make_async_remote_copy(
            src_ref=relay.at[source, st, a],
            dst_ref=arrived.at[quarter, pl.ds(2 * st, 2)],
            send_sem=pass_send.at[source, st, a], recv_sem=mir_recv.at[st, quarter],
            device_id=(4 * c + a, 2 * source + in_plane // 4), device_id_type=MESH,
        )

    def goes_round(st):
        return lax.rem(st, 2) == 0

    def is_relayed(st):
        return jnp.logical_and(off_diagonal, goes_round(st))

    def pass_on(st):
        @pl.when(jnp.logical_and(diagonal, goes_round(st)))
        def _():
            for k in range(1, 4):
                source = lax.rem(y + k, 4)
                block = relay.at[source, st]
                pltpu.make_async_copy(block, block, relay_recv.at[source, st]).wait()
                for turn in range(4):
                    pass_copy(source, st, lax.rem(turn + quarter, 4)).start()

    def update_into(ref, st):
        upd_t = dot(w_outer_t[...], outer_op[st])
        for k in range(6):
            ref[k] = upd_t[:, k * 128 : (k + 1) * 128].T

    def forward_step(st, upd, later):
        update_into(later, st + 1 if later is upd_odd else jnp.minimum(st + 1, 11))
        order = [(t, h) for t in range(2) for h in range(2)]
        finals = []
        for g in range(0, 4, FORWARD_GROUP):
            group = order[g : g + FORWARD_GROUP]
            ids = [2 * st + t + HALF * h for t, h in group]
            sums = []
            for (t, h), i in zip(group, ids):
                update = jnp.concatenate([upd[3 * t + h], upd[3 * t + 2][h * 64 : (h + 1) * 64]], axis=0)
                sums.append(permute(pair[i].astype(F32) + update, ORDER))
            mid = jnp.concatenate(sums, axis=0).astype(BF16)
            for n, i in enumerate(ids):
                middle[i] = mid[n * COLS : (n + 1) * COLS].reshape(3, CHUNK, 128)
            mid = mid.astype(F32)
            xn = normalize(mid)[0].astype(BF16)
            half = dot(xn, half_expand[...]).astype(BF16).astype(F32)
            th = jnp.tanh(half)
            hid = half + half * th
            slopes = ((1.0 + th) + (hid - hid * th)).astype(BF16)
            for n, i in enumerate(ids):
                slope[i] = slopes[n * COLS : (n + 1) * COLS].reshape(3, CHUNK, HID)
            final = (mid + dot(hid.astype(BF16), w_shrink[...])).astype(BF16)
            finals += [final[n * COLS : (n + 1) * COLS] for n in range(FORWARD_GROUP)]
        wide = jnp.concatenate(
            [jnp.concatenate(finals[0:2], axis=1), jnp.concatenate(finals[2:4], axis=1)], axis=0
        )
        logit = dot(wide, bins2[...]).astype(BF16)
        for t in range(2):
            for k in range(3):
                for a in range(4):
                    at = t * COLS + k * CHUNK + a * 16
                    logits[st, a, t, k] = logit[at : at + 16]

    def send_step(st):
        @pl.when(is_relayed(st))
        def _():
            relay_copy(st).start()

        @pl.when(jnp.logical_not(is_relayed(st)))
        def _():
            for turn in range(4):
                a = lax.rem(turn + quarter + y, 4)
                mine = mirror_is_self(a)

                @pl.when(mine)
                def _():
                    pltpu.make_async_copy(
                        logits.at[st, a],
                        arrived.at[quarter, pl.ds(2 * st, 2)],
                        mir_recv.at[st, quarter],
                    ).start()

                @pl.when(jnp.logical_not(mine))
                def _():
                    mirror_copy(st, a).start()

        @pl.when(st >= LAG)
        def _():
            pass_on(st - LAG)

    outer_block(0)
    update_into(upd_even, 0)

    def forward_pair(k, _):
        @pl.when(jnp.logical_or(k == 1, k == 3))
        def _():
            outer_block((k + 1) // 2)

        forward_step(2 * k, upd_even, upd_odd)
        send_step(2 * k)
        forward_step(2 * k + 1, upd_odd, upd_even)
        send_step(2 * k + 1)
        return 0

    lax.fori_loop(0, 6, forward_pair, 0)
    for st in range(12 - LAG, 12):
        pass_on(jnp.int32(st))

    def take_mirror(st, _):
        for s in range(4):
            rows = arrived.at[s, pl.ds(2 * st, 2)]
            pltpu.make_async_copy(rows, rows, mir_recv.at[st, s]).wait()
            for t in range(2):
                q = 2 * st + t
                block = arrived[s, q].reshape(ROWS, 128).astype(F32)
                mirror[pl.ds(pl.multiple_of(s * 1152 + q * ROWS, 16), ROWS), :] = block
        return 0

    span = BACK_ROWS * CHUNK
    first = lax.broadcasted_iota(jnp.int32, (span, 128), 1) < 64
    code = lax.rem(lax.broadcasted_iota(jnp.int32, (span, 128), 1), 64).astype(F32)
    first_chunk = lax.broadcasted_iota(jnp.int32, (CHUNK, 128), 1) < 64
    small = lax.broadcasted_iota(jnp.int32, (8, 128), 1) < 64
    sel_row = lax.broadcasted_iota(jnp.int32, (128, 256), 0)
    sel_lane = lax.broadcasted_iota(jnp.int32, (128, 256), 1)
    sel_add = HALF * lax.rem(sel_lane // 64, 2) + sel_lane // 128

    def backward_rows(k, g):
        col_weight = jnp.broadcast_to(goals[k][:, 48:49].astype(F32), (CHUNK, 128))
        parts, weights, aims, own = [], [], [], []
        for n in range(BACK_ROWS):
            p = BACK_ROWS * g + n
            for s in range(4):
                at = s * 1152 + k * (8 * ROWS) + (p // 8) * 16 + lax.rem(p, 8)
                x0 = mirror[pl.ds(at, 8, stride=ROWS), :]
                x1 = mirror[pl.ds(at + 8, 8, stride=ROWS), :]
                parts.append(jnp.where(small, x0, pltpu.roll(x1, 64, axis=1)))
                parts.append(jnp.where(small, pltpu.roll(x0, 64, axis=1), x1))
            m0 = mask[r * ROWS + p].astype(F32)
            m1 = mask[r * ROWS + p + HALF].astype(F32)
            weights.append(col_weight * jnp.where(first_chunk, m0, m1))
            own += [logits[p // 2, a, n % 2, k].astype(F32) for a in range(4)]
            if n % 2 == 0:
                both = dot(goals[k], (sel_row == sel_add + p).astype(BF16))
                aims += [both[:, :128], both[:, 128:]]
        scores = jnp.concatenate(own, axis=0) + jnp.concatenate(parts, axis=0)
        low_max = jnp.max(jnp.where(first, scores, -jnp.inf), axis=-1, keepdims=True)
        high_max = jnp.max(jnp.where(first, -jnp.inf, scores), axis=-1, keepdims=True)
        expo = jnp.exp(scores - jnp.where(first, low_max, high_max))
        low_sum = jnp.sum(jnp.where(first, expo, 0.0), axis=-1, keepdims=True)
        high_sum = jnp.sum(jnp.where(first, 0.0, expo), axis=-1, keepdims=True)
        prob = expo * jnp.where(first, 1.0 / low_sum, 1.0 / high_sum)
        aim = jnp.concatenate(aims, axis=0)
        dlog = ((prob - jnp.where(aim == code, 1.0, 0.0)) * jnp.concatenate(weights, axis=0)).astype(BF16)
        dfin = dot(dlog, bins2_t[...])
        ids = [BACK_ROWS * g + n + HALF * h for h in range(2) for n in range(BACK_ROWS)]
        grad = jnp.concatenate([dfin[:, :128], dfin[:, 128:]], axis=0)
        slopes = jnp.concatenate([slope[i, k] for i in ids], axis=0)
        dh = (dot(grad.astype(BF16), half_shrink_t[...]) * slopes.astype(F32)).astype(BF16)
        dxn = dot(dh, expand_t[...])
        mid = jnp.concatenate([middle[i, k] for i in ids], axis=0)
        xhat, scale = normalize(mid.astype(F32))
        overlap = jnp.mean(dxn * xhat, axis=-1, keepdims=True)
        res = (grad + scale * (dxn - xhat * overlap)).astype(BF16)
        for n, i in enumerate(ids):
            out[i, k] = res[n * CHUNK : (n + 1) * CHUNK]

    def backward_chunk(k, _):
        lax.fori_loop(4 * k, 4 * k + 4, take_mirror, 0)

        def backward_step(g, _):
            backward_rows(k, g)
            return 0

        lax.fori_loop(0, HALF // BACK_ROWS, backward_step, 0, unroll=BACK_UNROLL)
        return 0

    lax.fori_loop(0, 3, backward_chunk, 0)

    def drain_right(k, _):
        right_copy(r, k, partner).wait_send()
        return 0

    lax.fori_loop(0, 31, drain_right, 0)

    def drain_left(k, _):
        @pl.when(jnp.logical_not(left_self(k)))
        def _():
            left_copy(k).wait_send()

        return 0

    lax.fori_loop(0, 32, drain_left, 0)

    def drain_mirror(st, _):
        @pl.when(is_relayed(st))
        def _():
            relay_copy(st).wait_send()

        @pl.when(jnp.logical_not(is_relayed(st)))
        def _():
            for a in range(4):
                @pl.when(jnp.logical_not(mirror_is_self(a)))
                def _():
                    mirror_copy(st, a).wait_send()

        return 0

    lax.fori_loop(0, 12, drain_mirror, 0)

    def drain_pass(st, _):
        @pl.when(jnp.logical_and(diagonal, goes_round(st)))
        def _():
            for k in range(1, 4):
                for a in range(4):
                    pass_copy(lax.rem(y + k, 4), st, a).wait_send()

        return 0

    lax.fori_loop(0, 12, drain_pass, 0)


def unpermute(grads, out):
    for i in range(grads.shape[0]):
        out[i] = permute(grads[i].reshape(COLS, CH).astype(F32), BACK_ORDER).astype(BF16)


def per_device(
    alignment, pair_act, targets, crop_mask, projection_weight, w_outer, w_expand, w_shrink, w_bins
):
    vmem = pl.BlockSpec(memory_space=pltpu.VMEM)
    grads = pl.pallas_call(
        kernel,
        out_shape=jax.ShapeDtypeStruct((ROWS, 3, CHUNK, CH), BF16),
        in_specs=[vmem] * 4 + [pl.BlockSpec(memory_space=pltpu.SMEM)] + [vmem] * 5,
        out_specs=vmem,
        scratch_shapes=[
            pltpu.VMEM((32, 96, 128), BF16),
            pltpu.VMEM((32, 32, 128), BF16),
            pltpu.VMEM((4, 32, 128), BF16),
            pltpu.VMEM((3072, 128), F32),
            pltpu.VMEM((1024, 128), F32),
            pltpu.VMEM((768, 128), BF16),
            pltpu.VMEM((16, 3, 128, 256), BF16),
            pltpu.VMEM((12, 1024, 768), BF16),
            pltpu.VMEM((ROWS, 3, CHUNK, CH), BF16),
            pltpu.VMEM((ROWS, 3, CHUNK, HID), BF16),
            pltpu.VMEM((12, 4, 2, 3, 16, 128), BF16),
            pltpu.VMEM((4, HALF, 3, 16, 128), BF16),
            pltpu.VMEM((4 * HALF * ROWS, 128), F32),
            pltpu.VMEM((4, 12, 4, 2, 3, 16, 128), BF16),
            pltpu.VMEM((128, 1024), BF16),
            pltpu.VMEM((128, HID), BF16),
            pltpu.VMEM((256, 128), BF16),
            pltpu.VMEM((128, HID), BF16),
            pltpu.VMEM((HID, 128), BF16),
            pltpu.VMEM((128, 256), BF16),
            pltpu.VMEM((3, CHUNK, 128), BF16),
            pltpu.VMEM((6, 128, 128), F32),
            pltpu.VMEM((6, 128, 128), F32),
            pltpu.SemaphoreType.DMA((31,)),
            pltpu.SemaphoreType.DMA((32,)),
            pltpu.SemaphoreType.DMA((32,)),
            pltpu.SemaphoreType.DMA((32,)),
            pltpu.SemaphoreType.DMA((12, 4)),
            pltpu.SemaphoreType.DMA((12, 4)),
            pltpu.SemaphoreType.DMA((12,)),
            pltpu.SemaphoreType.DMA((4, 12)),
            pltpu.SemaphoreType.DMA((4, 12, 4)),
        ],
        compiler_params=pltpu.CompilerParams(
            collective_id=0, has_side_effects=True, vmem_limit_bytes=63 * 1024 * 1024
        ),
    )(
        alignment, pair_act, targets, crop_mask.reshape(12, 128), crop_mask, projection_weight.T,
        w_outer, w_expand, w_shrink, w_bins.T,
    )
    return pl.pallas_call(
        unpermute,
        grid=(ROWS // EMIT_ROWS,),
        out_shape=jax.ShapeDtypeStruct((ROWS, COLS, CH), BF16),
        in_specs=[pl.BlockSpec((EMIT_ROWS, 3, CHUNK, CH), lambda i: (i, 0, 0, 0))],
        out_specs=pl.BlockSpec((EMIT_ROWS, COLS, CH), lambda i: (i, 0, 0)),
    )(grads)


def solution(mesh):
    in_specs = (
        P("row", "col", None), P("row", "col", None), P("row", "col"),
        P(), P(), P(), P(), P(), P(),
    )
    return jax.shard_map(
        per_device, mesh=mesh, in_specs=in_specs, out_specs=P("row", "col", None), check_vma=False
    )
```

```python
import functools

import jax
import jax.numpy as jnp
from jax import lax
from jax.experimental import pallas as pl
from jax.experimental.pallas import tpu as pltpu
from jax.sharding import PartitionSpec as P

MESH = pl.DeviceIdType.MESH
F32 = jnp.float32
BF16 = jnp.bfloat16
EPS = 1e-05
ROWS, COLS, CH = 48, 192, 128
HALF = 24
HID = 512
OUTER_BLOCKS = 1
FORWARD_GROUP = 4
BACK_ROWS = 4
CHUNK = 64
EMIT_ROWS = 24
RELAYED = 6
LAG = 1
OUTER_UNROLL = 2
BACK_UNROLL = 3
ORDER = [a * 6 + h * 3 + k for k in range(3) for a in range(4) for h in range(2)]
BACK_ORDER = [ORDER.index(n) for n in range(24)]


def dot(a, b):
    return lax.dot_general(a, b, (((1,), (0,)), ((), ())), preferred_element_type=F32)


def permute(x, order):
    return jnp.concatenate([x[8 * n : 8 * n + 8] for n in order], axis=0)


def normalize(x):
    mean = jnp.mean(x, axis=-1, keepdims=True)
    centred = x - mean
    scale = lax.rsqrt(jnp.mean(centred * centred, axis=-1, keepdims=True) + EPS)
    return centred * scale, scale


def kernel(
    al, pair_hbm, targets, mask_rows, mask, pw_t, w_outer, w_expand, w_shrink, w_bins_t,
    out_hbm,
    g_right, g_left, own_left, f_right, f_left, left_op, right_op, outer_op, middle, slope, logits, arrived, mirror,
    relay, w_outer_t, half_expand, bins2, half_shrink_t, expand_t, bins2_t, goals, upd_even, upd_odd, pair, grads, pair_sem, out_sem,
    right_send, right_recv, left_send, left_recv, mir_send, mir_recv, relay_send, relay_recv, pass_send,
):
    r = lax.axis_index("row")
    c = lax.axis_index("col")
    z = lax.rem(r, 2)
    partner = r + 1 - 2 * z
    root = r // 4
    quarter = lax.rem(r, 4)
    y = r // 8
    diagonal = y == c // 2
    off_diagonal = jnp.logical_not(diagonal)
    in_plane = lax.rem(r, 8)

    pair_copy = pltpu.make_async_copy(pair_hbm, pair, pair_sem)
    pair_copy.start()

    bar = pltpu.get_barrier_semaphore()
    pl.semaphore_signal(bar, inc=1, device_id=(partner, c), device_id_type=MESH)

    def greet_plane(k, _):
        m = lax.rem(r // 2 + k, 16)
        pl.semaphore_signal(bar, inc=1, device_id=(2 * m + z, c), device_id_type=MESH)
        return 0

    lax.fori_loop(1, 16, greet_plane, 0)

    def greet_left(k, _):
        @pl.when(jnp.logical_or(k != r, root != c))
        def _():
            pl.semaphore_signal(bar, inc=1, device_id=(k, root), device_id_type=MESH)

        return 0

    lax.fori_loop(0, 32, greet_left, 0)
    for a in range(4):
        @pl.when(jnp.logical_or(4 * c + a != r, root != c))
        def _():
            pl.semaphore_signal(bar, inc=1, device_id=(4 * c + a, root), device_id_type=MESH)

    @pl.when(off_diagonal)
    def _():
        for s in range(4):
            pl.semaphore_signal(
                bar, inc=1, device_id=(8 * y + lax.rem(4 * c + s, 8), root), device_id_type=MESH
            )

    @pl.when(diagonal)
    def _():
        for k in range(1, 4):
            pl.semaphore_signal(
                bar, inc=1, device_id=(8 * lax.rem(y + k, 4) + in_plane, c), device_id_type=MESH
            )

    pw_right = pw_t[32:64, :]
    pw_left = pw_t[0:32, :].astype(F32)

    normed = []
    for s in range(2):
        normed.append(normalize(al[s].astype(F32))[0])
    tails = []
    for s in range(2):
        ft = lax.dot_general(
            pw_right, normed[s].astype(BF16), (((1,), (1,)), ((), ())), preferred_element_type=F32
        )
        g_right[r, pl.ds(32 * s, 32), :] = ft[:, :128].astype(BF16)
        tails.append(ft[:, 128:192])
    g_right[r, pl.ds(64, 32), :] = jnp.concatenate(tails, axis=1).astype(BF16)
    lf = None
    for h in range(2):
        for s in range(2):
            rows = jnp.concatenate(
                [normed[s][q * ROWS + h * HALF : q * ROWS + h * HALF + HALF] for q in range(4)], axis=0
            ).astype(BF16)
            before = 32 * (2 * h + s)
            place = [jnp.zeros((n, 256), F32) for n in (before, 96 - before) if n]
            place.insert(1 if before else 0, pw_left)
            place = jnp.concatenate(place, axis=0).astype(BF16)
            term = lax.dot_general(rows, place, (((1,), (1,)), ((), ())), preferred_element_type=F32)
            lf = term if lf is None else lf + term
    for q in range(4):
        own_left[q] = jnp.concatenate(
            [lf[q * HALF : (q + 1) * HALF], jnp.zeros((8, 128), F32)], axis=0
        ).astype(BF16)

    is_root = (root == c).astype(jnp.int32)
    on_diagonal = diagonal.astype(jnp.int32)
    pl.semaphore_wait(bar, 53 - 2 * is_root + 11 * on_diagonal)

    def right_copy(block, slot, dest):
        return pltpu.make_async_remote_copy(
            src_ref=g_right.at[block], dst_ref=g_right.at[block],
            send_sem=right_send.at[slot], recv_sem=right_recv.at[block],
            device_id=(dest, c), device_id_type=MESH,
        )

    right_copy(r, 0, partner).start()

    def start_own(k, _):
        m = lax.rem(r // 2 + k, 16)
        right_copy(r, k, 2 * m + z).start()
        return 0

    lax.fori_loop(1, 16, start_own, 0)

    def left_copy(k):
        return pltpu.make_async_remote_copy(
            src_ref=own_left.at[k // 8], dst_ref=g_left.at[r],
            send_sem=left_send.at[k], recv_sem=left_recv.at[r],
            device_id=(4 * c + k // 8, lax.rem(k, 8)), device_id_type=MESH,
        )

    def left_self(k):
        return jnp.logical_and(4 * c + k // 8 == r, lax.rem(k, 8) == c)

    def start_left(k, _):
        mine = left_self(k)

        @pl.when(mine)
        def _():
            pltpu.make_async_copy(own_left.at[k // 8], g_left.at[r], left_recv.at[r]).start()

        @pl.when(jnp.logical_not(mine))
        def _():
            left_copy(k).start()

        return 0

    lax.fori_loop(0, 32, start_left, 0)

    for k in range(4):
        cols = slice(k * 128, (k + 1) * 128)
        half_shrink_t[:, cols] = (0.5 * w_shrink[cols, :].astype(F32)).T.astype(BF16)
        wide = w_expand[:, cols].astype(F32)
        expand_t[cols, :] = (wide - jnp.mean(wide, axis=0, keepdims=True)).T.astype(BF16)
    half_expand[...] = (0.5 * w_expand[...].astype(F32)).astype(BF16)
    wb = jnp.concatenate([w_bins_t[...].astype(F32), jnp.zeros((64, 128), F32)], axis=0)
    wb_high = jnp.concatenate([jnp.zeros((64, 128), F32), w_bins_t[...].astype(F32)], axis=0)
    bins2[0:128, :] = wb.T.astype(BF16)
    bins2[128:256, :] = wb_high.T.astype(BF16)
    bins2_t[:, 0:128] = wb.astype(BF16)
    bins2_t[:, 128:256] = wb_high.astype(BF16)
    mirror[0:1024, :] = w_outer[...].astype(F32)
    for k in range(8):
        block = jnp.concatenate([mirror[pl.ds(4 * k + e, 32, stride=32), :] for e in range(4)], axis=0)
        w_outer_t[:, k * 128 : (k + 1) * 128] = block.T.astype(BF16)
    aims = targets[...].astype(F32)
    aims = [aims[:, :128], jnp.concatenate([aims[:, 128:], jnp.zeros((ROWS, 64), F32)], axis=1)]
    mask_a = mask_rows[pl.ds(3 * c // 2, 1), :].astype(F32)
    mask_b = mask_rows[pl.ds(3 * c // 2 + 1, 1), :].astype(F32)
    swap_a, swap_b = pltpu.roll(mask_a, 64, axis=1), pltpu.roll(mask_b, 64, axis=1)
    odd = jnp.broadcast_to(lax.rem(c, 2), (1, 128)) == 1
    low_lane = lax.broadcasted_iota(jnp.int32, (1, 128), 1) < 64
    masks = [
        jnp.where(odd, jnp.where(low_lane, swap_a, swap_b), mask_a),
        jnp.where(odd, swap_b, mask_b),
    ]
    table = [
        jnp.concatenate([x, 2.0 * m, jnp.zeros((79, 128), F32)], axis=0).T for x, m in zip(aims, masks)
    ]
    goals[...] = permute(
        jnp.concatenate([table[0], table[1][:64]], axis=0), ORDER
    ).astype(BF16).reshape(3, CHUNK, 128)

    right_copy(partner, 0, partner).wait_recv()

    def start_partner(k, _):
        m = lax.rem(r // 2 + k, 16)
        right_copy(partner, 15 + k, 2 * m + z).start()
        return 0

    lax.fori_loop(1, 16, start_partner, 0)

    def wait_left(k, _):
        pltpu.make_async_copy(g_left.at[k], g_left.at[k], left_recv.at[k]).wait()
        return 0

    lax.fori_loop(0, 32, wait_left, 0)

    def left_rows(k, _):
        f_left[pl.ds(pl.multiple_of(k * 32, 32), 32), :] = g_left[k].astype(F32) * (1.0 / 64.0)
        return 0

    lax.fori_loop(0, 32, left_rows, 0)

    def left_block(p, _):
        x = f_left[pl.ds(p, 32, stride=32), :]
        stack = jnp.concatenate([x] + [pltpu.roll(x, 128 - 32 * g, axis=1) for g in range(1, 4)], axis=0)
        left_op[pl.ds(pl.multiple_of(p * 32, 32), 32), :] = stack.T[:32].astype(BF16)
        return 0

    lax.fori_loop(0, HALF, left_block, 0)

    def take_right(block):
        f_right[pl.ds(pl.multiple_of(block * 96, 96), 96), :] = g_right[block].astype(F32)

    take_right(r)
    take_right(partner)

    def wait_right(k, _):
        m = lax.rem(r // 2 + k, 16)
        right_copy(2 * m + z, 0, partner).wait_recv()
        take_right(2 * m + z)
        return 0

    lax.fori_loop(1, 16, wait_right, 0)

    def wait_other(k, _):
        m = lax.rem(r // 2 + k, 16)
        right_copy(2 * m + 1 - z, 0, partner).wait_recv()
        take_right(2 * m + 1 - z)
        return 0

    lax.fori_loop(1, 16, wait_other, 0)

    low = lax.broadcasted_iota(jnp.int32, (32, 128), 1) < 64

    def right_chunks(e2):
        ab, tail = [], []
        zero = jnp.zeros((32, 128), F32)
        for par in range(2):
            e = 2 * e2 + par
            x0 = f_right[pl.ds(e, 32, stride=96), :]
            x1 = f_right[pl.ds(e + 32, 32, stride=96), :]
            xb = f_right[pl.ds(e + 64, 32, stride=96), :]
            xr = pltpu.roll(xb, 64, axis=1)
            h0 = jnp.concatenate([x0, x1, zero, zero], axis=0)
            h1 = jnp.concatenate([zero, zero, x0, x1], axis=0)
            ab.append(jnp.concatenate([h0, h1], axis=1).astype(BF16))
            tail.append(
                jnp.concatenate(
                    [
                        jnp.where(low, xb, zero), jnp.where(low, xr, zero),
                        jnp.where(low, zero, xr), jnp.where(low, zero, xb),
                    ],
                    axis=0,
                ).astype(BF16)
            )
        return ab + [jnp.concatenate(tail, axis=1)]

    def outer_rows(mb, e2, chunks):
        lhs = left_op[pl.ds(pl.multiple_of(mb * 128, 128), 128), :]
        for which in range(3):
            res = dot(lhs, chunks[which]).astype(BF16)
            for pi in range(4):
                pp = 2 * mb + pi // 2
                piece = res[pi * 32 : (pi + 1) * 32]
                if which < 2:
                    rows = pl.ds(pl.multiple_of((2 * e2 + which) * 32, 32), 32)
                    outer_op[pp, rows, pl.ds((pi % 2) * 384, 256)] = piece
                else:
                    for par in range(2):
                        rows = pl.ds(pl.multiple_of((2 * e2 + par) * 32, 32), 32)
                        outer_op[pp, rows, pl.ds((pi % 2) * 384 + 256, 128)] = piece[
                            :, par * 128 : (par + 1) * 128
                        ]

    def first_outer(e2, _):
        chunks = right_chunks(e2)
        for n in range(3):
            right_op[e2, n] = chunks[n]
        outer_rows(0, e2, chunks)
        return 0

    def outer_block(mb):
        def outer_step(e2, _):
            outer_rows(mb, e2, [right_op[e2, n] for n in range(3)])
            return 0

        lax.fori_loop(0, 16, outer_step, 0, unroll=OUTER_UNROLL)

    def mirror_copy(st, a):
        return pltpu.make_async_remote_copy(
            src_ref=logits.at[st, a],
            dst_ref=arrived.at[quarter, pl.ds(2 * st, 2)],
            send_sem=mir_send.at[st, a], recv_sem=mir_recv.at[st, quarter],
            device_id=(4 * c + a, root), device_id_type=MESH,
        )

    def mirror_is_self(a):
        return jnp.logical_and(4 * c + a == r, root == c)

    def relay_copy(st):
        return pltpu.make_async_remote_copy(
            src_ref=logits.at[st], dst_ref=relay.at[y, st],
            send_sem=relay_send.at[st], recv_sem=relay_recv.at[y, st],
            device_id=(8 * (c // 2) + in_plane, c), device_id_type=MESH,
        )

    def pass_copy(source, st, a):
        return pltpu.make_async_remote_copy(
            src_ref=relay.at[source, st, a],
            dst_ref=arrived.at[quarter, pl.ds(2 * st, 2)],
            send_sem=pass_send.at[source, st, a], recv_sem=mir_recv.at[st, quarter],
            device_id=(4 * c + a, 2 * source + in_plane // 4), device_id_type=MESH,
        )

    def goes_round(st):
        return lax.rem(st, 2) == 0

    def is_relayed(st):
        return jnp.logical_and(off_diagonal, goes_round(st))

    def pass_on(st):
        @pl.when(jnp.logical_and(diagonal, goes_round(st)))
        def _():
            for k in range(1, 4):
                source = lax.rem(y + k, 4)
                block = relay.at[source, st]
                pltpu.make_async_copy(block, block, relay_recv.at[source, st]).wait()
                for turn in range(4):
                    pass_copy(source, st, lax.rem(turn + quarter, 4)).start()

    def update_into(ref, st):
        upd_t = dot(w_outer_t[...], outer_op[st])
        for k in range(6):
            ref[k] = upd_t[:, k * 128 : (k + 1) * 128].T

    def forward_step(st, upd, later):
        update_into(later, st + 1 if later is upd_odd else jnp.minimum(st + 1, 11))
        order = [(t, h) for t in range(2) for h in range(2)]
        finals = []
        for g in range(0, 4, FORWARD_GROUP):
            group = order[g : g + FORWARD_GROUP]
            ids = [2 * st + t + HALF * h for t, h in group]
            sums = []
            for (t, h), i in zip(group, ids):
                update = jnp.concatenate([upd[3 * t + h], upd[3 * t + 2][h * 64 : (h + 1) * 64]], axis=0)
                sums.append(permute(pair[i].astype(F32) + update, ORDER))
            mid = jnp.concatenate(sums, axis=0).astype(BF16)
            for n, i in enumerate(ids):
                middle[i] = mid[n * COLS : (n + 1) * COLS].reshape(3, CHUNK, 128)
            mid = mid.astype(F32)
            xn = normalize(mid)[0].astype(BF16)
            half = dot(xn, half_expand[...]).astype(BF16).astype(F32)
            th = jnp.tanh(half)
            hid = half + half * th
            slopes = ((1.0 + th) + (hid - hid * th)).astype(BF16)
            for n, i in enumerate(ids):
                slope[i] = slopes[n * COLS : (n + 1) * COLS].reshape(3, CHUNK, HID)
            final = (mid + dot(hid.astype(BF16), w_shrink[...])).astype(BF16)
            finals += [final[n * COLS : (n + 1) * COLS] for n in range(FORWARD_GROUP)]
        wide = jnp.concatenate(
            [jnp.concatenate(finals[0:2], axis=1), jnp.concatenate(finals[2:4], axis=1)], axis=0
        )
        logit = dot(wide, bins2[...]).astype(BF16)
        for t in range(2):
            for k in range(3):
                for a in range(4):
                    at = t * COLS + k * CHUNK + a * 16
                    logits[st, a, t, k] = logit[at : at + 16]

    def send_step(st):
        @pl.when(is_relayed(st))
        def _():
            relay_copy(st).start()

        @pl.when(jnp.logical_not(is_relayed(st)))
        def _():
            for turn in range(4):
                a = lax.rem(turn + quarter + y, 4)
                mine = mirror_is_self(a)

                @pl.when(mine)
                def _():
                    pltpu.make_async_copy(
                        logits.at[st, a],
                        arrived.at[quarter, pl.ds(2 * st, 2)],
                        mir_recv.at[st, quarter],
                    ).start()

                @pl.when(jnp.logical_not(mine))
                def _():
                    mirror_copy(st, a).start()

        @pl.when(st >= LAG)
        def _():
            pass_on(st - LAG)

    lax.fori_loop(0, 16, first_outer, 0, unroll=OUTER_UNROLL)
    pair_copy.wait()
    update_into(upd_even, 0)

    def forward_pair(k, _):
        forward_step(2 * k, upd_even, upd_odd)
        send_step(2 * k)

        @pl.when(k < 5)
        def _():
            outer_block(k + 1)

        forward_step(2 * k + 1, upd_odd, upd_even)
        send_step(2 * k + 1)
        return 0

    lax.fori_loop(0, 6, forward_pair, 0)
    for st in range(12 - LAG, 12):
        pass_on(jnp.int32(st))

    def take_mirror(st, _):
        for s in range(4):
            rows = arrived.at[s, pl.ds(2 * st, 2)]
            pltpu.make_async_copy(rows, rows, mir_recv.at[st, s]).wait()
            for t in range(2):
                q = 2 * st + t
                block = arrived[s, q].reshape(ROWS, 128).astype(F32)
                mirror[pl.ds(pl.multiple_of(s * 1152 + q * ROWS, 16), ROWS), :] = block
        return 0

    span = BACK_ROWS * CHUNK
    first = lax.broadcasted_iota(jnp.int32, (span, 128), 1) < 64
    code = lax.rem(lax.broadcasted_iota(jnp.int32, (span, 128), 1), 64).astype(F32)
    first_chunk = lax.broadcasted_iota(jnp.int32, (CHUNK, 128), 1) < 64
    small = lax.broadcasted_iota(jnp.int32, (8, 128), 1) < 64
    sel_row = lax.broadcasted_iota(jnp.int32, (128, 256), 0)
    sel_lane = lax.broadcasted_iota(jnp.int32, (128, 256), 1)
    sel_add = HALF * lax.rem(sel_lane // 64, 2) + sel_lane // 128

    def backward_rows(k, g):
        col_weight = jnp.broadcast_to(goals[k][:, 48:49].astype(F32), (CHUNK, 128))
        parts, weights, aims, own = [], [], [], []
        for n in range(BACK_ROWS):
            p = BACK_ROWS * g + n
            for s in range(4):
                at = s * 1152 + k * (8 * ROWS) + (p // 8) * 16 + lax.rem(p, 8)
                x0 = mirror[pl.ds(at, 8, stride=ROWS), :]
                x1 = mirror[pl.ds(at + 8, 8, stride=ROWS), :]
                parts.append(jnp.where(small, x0, pltpu.roll(x1, 64, axis=1)))
                parts.append(jnp.where(small, pltpu.roll(x0, 64, axis=1), x1))
            m0 = mask[r * ROWS + p].astype(F32)
            m1 = mask[r * ROWS + p + HALF].astype(F32)
            weights.append(col_weight * jnp.where(first_chunk, m0, m1))
            own += [logits[p // 2, a, n % 2, k].astype(F32) for a in range(4)]
            if n % 2 == 0:
                both = dot(goals[k], (sel_row == sel_add + p).astype(BF16))
                aims += [both[:, :128], both[:, 128:]]
        scores = jnp.concatenate(own, axis=0) + jnp.concatenate(parts, axis=0)
        low_max = jnp.max(jnp.where(first, scores, -jnp.inf), axis=-1, keepdims=True)
        high_max = jnp.max(jnp.where(first, -jnp.inf, scores), axis=-1, keepdims=True)
        expo = jnp.exp(scores - jnp.where(first, low_max, high_max))
        low_sum = jnp.sum(jnp.where(first, expo, 0.0), axis=-1, keepdims=True)
        high_sum = jnp.sum(jnp.where(first, 0.0, expo), axis=-1, keepdims=True)
        prob = expo * jnp.where(first, 1.0 / low_sum, 1.0 / high_sum)
        aim = jnp.concatenate(aims, axis=0)
        dlog = ((prob - jnp.where(aim == code, 1.0, 0.0)) * jnp.concatenate(weights, axis=0)).astype(BF16)
        dfin = dot(dlog, bins2_t[...])
        ids = [BACK_ROWS * g + n + HALF * h for h in range(2) for n in range(BACK_ROWS)]
        grad = jnp.concatenate([dfin[:, :128], dfin[:, 128:]], axis=0)
        slopes = jnp.concatenate([slope[i, k] for i in ids], axis=0)
        dh = (dot(grad.astype(BF16), half_shrink_t[...]) * slopes.astype(F32)).astype(BF16)
        dxn = dot(dh, expand_t[...])
        mid = jnp.concatenate([middle[i, k] for i in ids], axis=0)
        xhat, scale = normalize(mid.astype(F32))
        overlap = jnp.mean(dxn * xhat, axis=-1, keepdims=True)
        res = (grad + scale * (dxn - xhat * overlap)).astype(BF16)
        for n, i in enumerate(ids):
            grads[k, i] = res[n * CHUNK : (n + 1) * CHUNK]

    def backward_chunk(k, _):
        lax.fori_loop(4 * k, 4 * k + 4, take_mirror, 0)

        def backward_step(g, _):
            backward_rows(k, g)
            return 0

        lax.fori_loop(0, HALF // BACK_ROWS, backward_step, 0, unroll=BACK_UNROLL)
        pltpu.make_async_copy(grads.at[k], out_hbm.at[k], out_sem.at[k]).start()
        return 0

    lax.fori_loop(0, 3, backward_chunk, 0)

    for k in range(3):
        pltpu.make_async_copy(grads.at[k], out_hbm.at[k], out_sem.at[k]).wait()

    def drain_right(k, _):
        right_copy(r, k, partner).wait_send()
        return 0

    lax.fori_loop(0, 31, drain_right, 0)

    def drain_left(k, _):
        @pl.when(jnp.logical_not(left_self(k)))
        def _():
            left_copy(k).wait_send()

        return 0

    lax.fori_loop(0, 32, drain_left, 0)

    def drain_mirror(st, _):
        @pl.when(is_relayed(st))
        def _():
            relay_copy(st).wait_send()

        @pl.when(jnp.logical_not(is_relayed(st)))
        def _():
            for a in range(4):
                @pl.when(jnp.logical_not(mirror_is_self(a)))
                def _():
                    mirror_copy(st, a).wait_send()

        return 0

    lax.fori_loop(0, 12, drain_mirror, 0)

    def drain_pass(st, _):
        @pl.when(jnp.logical_and(diagonal, goes_round(st)))
        def _():
            for k in range(1, 4):
                for a in range(4):
                    pass_copy(lax.rem(y + k, 4), st, a).wait_send()

        return 0

    lax.fori_loop(0, 12, drain_pass, 0)


def unpermute(grads, out):
    for i in range(out.shape[0]):
        rows = jnp.concatenate([grads[k, i].astype(F32) for k in range(3)], axis=0)
        out[i] = permute(rows, BACK_ORDER).astype(BF16)


def per_device(
    alignment, pair_act, targets, crop_mask, projection_weight, w_outer, w_expand, w_shrink, w_bins
):
    vmem = pl.BlockSpec(memory_space=pltpu.VMEM)
    anywhere = pl.BlockSpec(memory_space=pl.ANY)
    grads = pl.pallas_call(
        kernel,
        out_shape=jax.ShapeDtypeStruct((3, ROWS, CHUNK, CH), BF16),
        in_specs=[vmem, anywhere, vmem, vmem] + [pl.BlockSpec(memory_space=pltpu.SMEM)] + [vmem] * 5,
        out_specs=anywhere,
        scratch_shapes=[
            pltpu.VMEM((32, 96, 128), BF16),
            pltpu.VMEM((32, 32, 128), BF16),
            pltpu.VMEM((4, 32, 128), BF16),
            pltpu.VMEM((3072, 128), F32),
            pltpu.VMEM((1024, 128), F32),
            pltpu.VMEM((768, 128), BF16),
            pltpu.VMEM((16, 3, 128, 256), BF16),
            pltpu.VMEM((12, 1024, 768), BF16),
            pltpu.VMEM((ROWS, 3, CHUNK, CH), BF16),
            pltpu.VMEM((ROWS, 3, CHUNK, HID), BF16),
            pltpu.VMEM((12, 4, 2, 3, 16, 128), BF16),
            pltpu.VMEM((4, HALF, 3, 16, 128), BF16),
            pltpu.VMEM((4 * HALF * ROWS, 128), F32),
            pltpu.VMEM((4, 12, 4, 2, 3, 16, 128), BF16),
            pltpu.VMEM((128, 1024), BF16),
            pltpu.VMEM((128, HID), BF16),
            pltpu.VMEM((256, 128), BF16),
            pltpu.VMEM((128, HID), BF16),
            pltpu.VMEM((HID, 128), BF16),
            pltpu.VMEM((128, 256), BF16),
            pltpu.VMEM((3, CHUNK, 128), BF16),
            pltpu.VMEM((6, 128, 128), F32),
            pltpu.VMEM((6, 128, 128), F32),
            pltpu.VMEM((ROWS, COLS, CH), BF16),
            pltpu.VMEM((3, ROWS, CHUNK, CH), BF16),
            pltpu.SemaphoreType.DMA(()),
            pltpu.SemaphoreType.DMA((3,)),
            pltpu.SemaphoreType.DMA((31,)),
            pltpu.SemaphoreType.DMA((32,)),
            pltpu.SemaphoreType.DMA((32,)),
            pltpu.SemaphoreType.DMA((32,)),
            pltpu.SemaphoreType.DMA((12, 4)),
            pltpu.SemaphoreType.DMA((12, 4)),
            pltpu.SemaphoreType.DMA((12,)),
            pltpu.SemaphoreType.DMA((4, 12)),
            pltpu.SemaphoreType.DMA((4, 12, 4)),
        ],
        compiler_params=pltpu.CompilerParams(
            collective_id=0, has_side_effects=True, vmem_limit_bytes=63 * 1024 * 1024
        ),
    )(
        alignment, pair_act, targets, crop_mask.reshape(12, 128), crop_mask, projection_weight.T,
        w_outer, w_expand, w_shrink, w_bins.T,
    )
    return pl.pallas_call(
        unpermute,
        grid=(ROWS // EMIT_ROWS,),
        out_shape=jax.ShapeDtypeStruct((ROWS, COLS, CH), BF16),
        in_specs=[pl.BlockSpec((3, EMIT_ROWS, CHUNK, CH), lambda i: (0, i, 0, 0))],
        out_specs=pl.BlockSpec((EMIT_ROWS, COLS, CH), lambda i: (i, 0, 0)),
    )(grads)


def solution(mesh):
    in_specs = (
        P("row", "col", None), P("row", "col", None), P("row", "col"),
        P(), P(), P(), P(), P(), P(),
    )
    return jax.shard_map(
        per_device, mesh=mesh, in_specs=in_specs, out_specs=P("row", "col", None), check_vma=False
    )
```

```python
import functools

import jax
import jax.numpy as jnp
from jax import lax
from jax.experimental import pallas as pl
from jax.experimental.pallas import tpu as pltpu
from jax.sharding import PartitionSpec as P

MESH = pl.DeviceIdType.MESH
F32 = jnp.float32
BF16 = jnp.bfloat16
EPS = 1e-05
ROWS, COLS, CH = 48, 192, 128
HALF = 24
HID = 512
OUTER_BLOCKS = 1
FORWARD_GROUP = 4
BACK_ROWS = 4
CHUNK = 64
EMIT_ROWS = 24
RELAYED = 6
LAG = 1
OUTER_UNROLL = 2
BACK_UNROLL = 3
ORDER = [a * 6 + h * 3 + k for k in range(3) for a in range(4) for h in range(2)]
BACK_ORDER = [ORDER.index(n) for n in range(24)]


def dot(a, b):
    return lax.dot_general(a, b, (((1,), (0,)), ((), ())), preferred_element_type=F32)


def permute(x, order):
    return jnp.concatenate([x[8 * n : 8 * n + 8] for n in order], axis=0)


def normalize(x):
    mean = jnp.mean(x, axis=-1, keepdims=True)
    centred = x - mean
    scale = lax.rsqrt(jnp.mean(centred * centred, axis=-1, keepdims=True) + EPS)
    return centred * scale, scale


def kernel(
    al, pair_hbm, targets, mask_rows, mask, pw_t, w_outer, w_expand, w_shrink, w_bins_t,
    out_hbm,
    g_right, g_left, own_left, f_right, f_left, left_op, right_op, outer_op, middle, slope, logits, arrived, mirror,
    relay, w_outer_t, half_expand, bins2, half_shrink_t, expand_t, bins2_t, goals, upd_even, upd_odd, pair, grads, pair_sem, out_sem,
    right_send, right_recv, left_send, left_recv, mir_send, mir_recv, relay_send, relay_recv, pass_send,
):
    r = lax.axis_index("row")
    c = lax.axis_index("col")
    z = lax.rem(r, 2)
    partner = r + 1 - 2 * z
    root = r // 4
    quarter = lax.rem(r, 4)
    y = r // 8
    diagonal = y == c // 2
    off_diagonal = jnp.logical_not(diagonal)
    in_plane = lax.rem(r, 8)

    pair_copy = pltpu.make_async_copy(pair_hbm, pair, pair_sem)
    pair_copy.start()

    bar = pltpu.get_barrier_semaphore()
    pl.semaphore_signal(bar, inc=1, device_id=(partner, c), device_id_type=MESH)

    def greet_plane(k, _):
        m = lax.rem(r // 2 + k, 16)
        pl.semaphore_signal(bar, inc=1, device_id=(2 * m + z, c), device_id_type=MESH)
        return 0

    lax.fori_loop(1, 16, greet_plane, 0)

    def greet_left(k, _):
        @pl.when(jnp.logical_or(k != r, root != c))
        def _():
            pl.semaphore_signal(bar, inc=1, device_id=(k, root), device_id_type=MESH)

        return 0

    lax.fori_loop(0, 32, greet_left, 0)
    for a in range(4):
        @pl.when(jnp.logical_or(4 * c + a != r, root != c))
        def _():
            pl.semaphore_signal(bar, inc=1, device_id=(4 * c + a, root), device_id_type=MESH)

    @pl.when(off_diagonal)
    def _():
        for s in range(4):
            pl.semaphore_signal(
                bar, inc=1, device_id=(8 * y + lax.rem(4 * c + s, 8), root), device_id_type=MESH
            )

    @pl.when(diagonal)
    def _():
        for k in range(1, 4):
            pl.semaphore_signal(
                bar, inc=1, device_id=(8 * lax.rem(y + k, 4) + in_plane, c), device_id_type=MESH
            )

    pw_right = pw_t[32:64, :]
    pw_left = pw_t[0:32, :].astype(F32)

    normed = []
    for s in range(2):
        normed.append(normalize(al[s].astype(F32))[0])
    tails = []
    for s in range(2):
        ft = lax.dot_general(
            pw_right, normed[s].astype(BF16), (((1,), (1,)), ((), ())), preferred_element_type=F32
        )
        g_right[r, pl.ds(32 * s, 32), :] = ft[:, :128].astype(BF16)
        tails.append(ft[:, 128:192])
    g_right[r, pl.ds(64, 32), :] = jnp.concatenate(tails, axis=1).astype(BF16)
    lf = None
    for h in range(2):
        for s in range(2):
            rows = jnp.concatenate(
                [normed[s][q * ROWS + h * HALF : q * ROWS + h * HALF + HALF] for q in range(4)], axis=0
            ).astype(BF16)
            before = 32 * (2 * h + s)
            place = [jnp.zeros((n, 256), F32) for n in (before, 96 - before) if n]
            place.insert(1 if before else 0, pw_left)
            place = jnp.concatenate(place, axis=0).astype(BF16)
            term = lax.dot_general(rows, place, (((1,), (1,)), ((), ())), preferred_element_type=F32)
            lf = term if lf is None else lf + term
    for q in range(4):
        own_left[q] = jnp.concatenate(
            [lf[q * HALF : (q + 1) * HALF], jnp.zeros((8, 128), F32)], axis=0
        ).astype(BF16)

    is_root = (root == c).astype(jnp.int32)
    on_diagonal = diagonal.astype(jnp.int32)
    pl.semaphore_wait(bar, 53 - 2 * is_root + 11 * on_diagonal)

    def right_copy(block, slot, dest):
        return pltpu.make_async_remote_copy(
            src_ref=g_right.at[block], dst_ref=g_right.at[block],
            send_sem=right_send.at[slot], recv_sem=right_recv.at[block],
            device_id=(dest, c), device_id_type=MESH,
        )

    right_copy(r, 0, partner).start()

    def start_own(k, _):
        m = lax.rem(r // 2 + k, 16)
        right_copy(r, k, 2 * m + z).start()
        return 0

    lax.fori_loop(1, 16, start_own, 0)

    def left_copy(k):
        return pltpu.make_async_remote_copy(
            src_ref=own_left.at[k // 8], dst_ref=g_left.at[r],
            send_sem=left_send.at[k], recv_sem=left_recv.at[r],
            device_id=(4 * c + k // 8, lax.rem(k, 8)), device_id_type=MESH,
        )

    def left_self(k):
        return jnp.logical_and(4 * c + k // 8 == r, lax.rem(k, 8) == c)

    def start_left(k, _):
        mine = left_self(k)

        @pl.when(mine)
        def _():
            pltpu.make_async_copy(own_left.at[k // 8], g_left.at[r], left_recv.at[r]).start()

        @pl.when(jnp.logical_not(mine))
        def _():
            left_copy(k).start()

        return 0

    lax.fori_loop(0, 32, start_left, 0)

    for k in range(4):
        cols = slice(k * 128, (k + 1) * 128)
        half_shrink_t[:, cols] = (0.5 * w_shrink[cols, :].astype(F32)).T.astype(BF16)
        wide = w_expand[:, cols].astype(F32)
        expand_t[cols, :] = (wide - jnp.mean(wide, axis=0, keepdims=True)).T.astype(BF16)
    half_expand[...] = (0.5 * w_expand[...].astype(F32)).astype(BF16)
    wb = jnp.concatenate([w_bins_t[...].astype(F32), jnp.zeros((64, 128), F32)], axis=0)
    wb_high = jnp.concatenate([jnp.zeros((64, 128), F32), w_bins_t[...].astype(F32)], axis=0)
    bins2[0:128, :] = wb.T.astype(BF16)
    bins2[128:256, :] = wb_high.T.astype(BF16)
    bins2_t[:, 0:128] = wb.astype(BF16)
    bins2_t[:, 128:256] = wb_high.astype(BF16)
    mirror[0:1024, :] = w_outer[...].astype(F32)
    for k in range(8):
        block = jnp.concatenate([mirror[pl.ds(4 * k + e, 32, stride=32), :] for e in range(4)], axis=0)
        w_outer_t[:, k * 128 : (k + 1) * 128] = block.T.astype(BF16)
    aims = targets[...].astype(F32)
    aims = [aims[:, :128], jnp.concatenate([aims[:, 128:], jnp.zeros((ROWS, 64), F32)], axis=1)]
    mask_a = mask_rows[pl.ds(3 * c // 2, 1), :].astype(F32)
    mask_b = mask_rows[pl.ds(3 * c // 2 + 1, 1), :].astype(F32)
    swap_a, swap_b = pltpu.roll(mask_a, 64, axis=1), pltpu.roll(mask_b, 64, axis=1)
    odd = jnp.broadcast_to(lax.rem(c, 2), (1, 128)) == 1
    low_lane = lax.broadcasted_iota(jnp.int32, (1, 128), 1) < 64
    masks = [
        jnp.where(odd, jnp.where(low_lane, swap_a, swap_b), mask_a),
        jnp.where(odd, swap_b, mask_b),
    ]
    table = [
        jnp.concatenate([x, 2.0 * m, jnp.zeros((79, 128), F32)], axis=0).T for x, m in zip(aims, masks)
    ]
    goals[...] = permute(
        jnp.concatenate([table[0], table[1][:64]], axis=0), ORDER
    ).astype(BF16).reshape(3, CHUNK, 128)

    right_copy(partner, 0, partner).wait_recv()

    def start_partner(k, _):
        m = lax.rem(r // 2 + k, 16)
        right_copy(partner, 15 + k, 2 * m + z).start()
        return 0

    lax.fori_loop(1, 16, start_partner, 0)

    def wait_left(k, _):
        pltpu.make_async_copy(g_left.at[k], g_left.at[k], left_recv.at[k]).wait()
        return 0

    lax.fori_loop(0, 32, wait_left, 0)

    def left_rows(k, _):
        f_left[pl.ds(pl.multiple_of(k * 32, 32), 32), :] = g_left[k].astype(F32) * (1.0 / 64.0)
        return 0

    lax.fori_loop(0, 32, left_rows, 0)

    def left_block(p, _):
        x = f_left[pl.ds(p, 32, stride=32), :]
        stack = jnp.concatenate([x] + [pltpu.roll(x, 128 - 32 * g, axis=1) for g in range(1, 4)], axis=0)
        left_op[pl.ds(pl.multiple_of(p * 32, 32), 32), :] = stack.T[:32].astype(BF16)
        return 0

    lax.fori_loop(0, HALF, left_block, 0)

    def take_right(block):
        f_right[pl.ds(pl.multiple_of(block * 96, 96), 96), :] = g_right[block].astype(F32)

    take_right(r)
    take_right(partner)

    def wait_right(k, _):
        m = lax.rem(r // 2 + k, 16)
        right_copy(2 * m + z, 0, partner).wait_recv()
        take_right(2 * m + z)
        return 0

    lax.fori_loop(1, 16, wait_right, 0)

    def wait_other(k, _):
        m = lax.rem(r // 2 + k, 16)
        right_copy(2 * m + 1 - z, 0, partner).wait_recv()
        take_right(2 * m + 1 - z)
        return 0

    lax.fori_loop(1, 16, wait_other, 0)

    low = lax.broadcasted_iota(jnp.int32, (32, 128), 1) < 64

    def right_chunks(e2):
        ab, tail = [], []
        zero = jnp.zeros((32, 128), F32)
        for par in range(2):
            e = 2 * e2 + par
            x0 = f_right[pl.ds(e, 32, stride=96), :]
            x1 = f_right[pl.ds(e + 32, 32, stride=96), :]
            xb = f_right[pl.ds(e + 64, 32, stride=96), :]
            xr = pltpu.roll(xb, 64, axis=1)
            h0 = jnp.concatenate([x0, x1, zero, zero], axis=0)
            h1 = jnp.concatenate([zero, zero, x0, x1], axis=0)
            ab.append(jnp.concatenate([h0, h1], axis=1).astype(BF16))
            tail.append(
                jnp.concatenate(
                    [
                        jnp.where(low, xb, zero), jnp.where(low, xr, zero),
                        jnp.where(low, zero, xr), jnp.where(low, zero, xb),
                    ],
                    axis=0,
                ).astype(BF16)
            )
        return ab + [jnp.concatenate(tail, axis=1)]

    def outer_rows(mb, e2, chunks):
        lhs = left_op[pl.ds(pl.multiple_of(mb * 128, 128), 128), :]
        for which in range(3):
            res = dot(lhs, chunks[which]).astype(BF16)
            for pi in range(4):
                pp = 2 * mb + pi // 2
                piece = res[pi * 32 : (pi + 1) * 32]
                if which < 2:
                    rows = pl.ds(pl.multiple_of((2 * e2 + which) * 32, 32), 32)
                    outer_op[pp, rows, pl.ds((pi % 2) * 384, 256)] = piece
                else:
                    for par in range(2):
                        rows = pl.ds(pl.multiple_of((2 * e2 + par) * 32, 32), 32)
                        outer_op[pp, rows, pl.ds((pi % 2) * 384 + 256, 128)] = piece[
                            :, par * 128 : (par + 1) * 128
                        ]

    def first_outer(e2, _):
        chunks = right_chunks(e2)
        for n in range(3):
            right_op[e2, n] = chunks[n]
        outer_rows(0, e2, chunks)
        return 0

    def outer_block(mb):
        def outer_step(e2, _):
            outer_rows(mb, e2, [right_op[e2, n] for n in range(3)])
            return 0

        lax.fori_loop(0, 16, outer_step, 0, unroll=4)

    def mirror_copy(st, a):
        return pltpu.make_async_remote_copy(
            src_ref=logits.at[st, a],
            dst_ref=arrived.at[quarter, pl.ds(2 * st, 2)],
            send_sem=mir_send.at[st, a], recv_sem=mir_recv.at[st, quarter],
            device_id=(4 * c + a, root), device_id_type=MESH,
        )

    def mirror_is_self(a):
        return jnp.logical_and(4 * c + a == r, root == c)

    def relay_copy(st):
        return pltpu.make_async_remote_copy(
            src_ref=logits.at[st], dst_ref=relay.at[y, st],
            send_sem=relay_send.at[st], recv_sem=relay_recv.at[y, st],
            device_id=(8 * (c // 2) + in_plane, c), device_id_type=MESH,
        )

    def pass_copy(source, st, a):
        return pltpu.make_async_remote_copy(
            src_ref=relay.at[source, st, a],
            dst_ref=arrived.at[quarter, pl.ds(2 * st, 2)],
            send_sem=pass_send.at[source, st, a], recv_sem=mir_recv.at[st, quarter],
            device_id=(4 * c + a, 2 * source + in_plane // 4), device_id_type=MESH,
        )

    def goes_round(st):
        return lax.rem(st, 2) == 0

    def is_relayed(st):
        return jnp.logical_and(off_diagonal, goes_round(st))

    def pass_on(st):
        @pl.when(jnp.logical_and(diagonal, goes_round(st)))
        def _():
            for k in range(1, 4):
                source = lax.rem(y + k, 4)
                block = relay.at[source, st]
                pltpu.make_async_copy(block, block, relay_recv.at[source, st]).wait()
                for turn in range(4):
                    pass_copy(source, st, lax.rem(turn + quarter, 4)).start()

    def update_into(ref, st):
        upd_t = dot(w_outer_t[...], outer_op[st])
        for k in range(6):
            ref[k] = upd_t[:, k * 128 : (k + 1) * 128].T

    def forward_step(st, upd, later):
        update_into(later, st + 1 if later is upd_odd else jnp.minimum(st + 1, 11))
        order = [(t, h) for t in range(2) for h in range(2)]
        finals = []
        for g in range(0, 4, FORWARD_GROUP):
            group = order[g : g + FORWARD_GROUP]
            ids = [2 * st + t + HALF * h for t, h in group]
            sums = []
            for (t, h), i in zip(group, ids):
                update = jnp.concatenate([upd[3 * t + h], upd[3 * t + 2][h * 64 : (h + 1) * 64]], axis=0)
                sums.append(permute(pair[i].astype(F32) + update, ORDER))
            mid = jnp.concatenate(sums, axis=0).astype(BF16)
            for n, i in enumerate(ids):
                middle[i] = mid[n * COLS : (n + 1) * COLS].reshape(3, CHUNK, 128)
            mid = mid.astype(F32)
            xn = normalize(mid)[0].astype(BF16)
            half = dot(xn, half_expand[...]).astype(BF16).astype(F32)
            th = jnp.tanh(half)
            hid = half + half * th
            slopes = ((1.0 + th) + (hid - hid * th)).astype(BF16)
            for n, i in enumerate(ids):
                slope[i] = slopes[n * COLS : (n + 1) * COLS].reshape(3, CHUNK, HID)
            final = (mid + dot(hid.astype(BF16), w_shrink[...])).astype(BF16)
            finals += [final[n * COLS : (n + 1) * COLS] for n in range(FORWARD_GROUP)]
        wide = jnp.concatenate(
            [jnp.concatenate(finals[0:2], axis=1), jnp.concatenate(finals[2:4], axis=1)], axis=0
        )
        logit = dot(wide, bins2[...]).astype(BF16)
        for t in range(2):
            for k in range(3):
                for a in range(4):
                    at = t * COLS + k * CHUNK + a * 16
                    logits[st, a, t, k] = logit[at : at + 16]

    def send_step(st):
        @pl.when(is_relayed(st))
        def _():
            relay_copy(st).start()

        @pl.when(jnp.logical_not(is_relayed(st)))
        def _():
            for turn in range(4):
                a = lax.rem(turn + quarter + y, 4)
                mine = mirror_is_self(a)

                @pl.when(mine)
                def _():
                    pltpu.make_async_copy(
                        logits.at[st, a],
                        arrived.at[quarter, pl.ds(2 * st, 2)],
                        mir_recv.at[st, quarter],
                    ).start()

                @pl.when(jnp.logical_not(mine))
                def _():
                    mirror_copy(st, a).start()

        @pl.when(st >= LAG)
        def _():
            pass_on(st - LAG)

    lax.fori_loop(0, 16, first_outer, 0, unroll=4)
    pair_copy.wait()
    update_into(upd_even, 0)

    def forward_pair(k, _):
        forward_step(2 * k, upd_even, upd_odd)
        send_step(2 * k)

        @pl.when(k < 5)
        def _():
            outer_block(k + 1)

        forward_step(2 * k + 1, upd_odd, upd_even)
        send_step(2 * k + 1)
        return 0

    lax.fori_loop(0, 6, forward_pair, 0)
    for st in range(12 - LAG, 12):
        pass_on(jnp.int32(st))

    def take_mirror(st, _):
        for s in range(4):
            rows = arrived.at[s, pl.ds(2 * st, 2)]
            pltpu.make_async_copy(rows, rows, mir_recv.at[st, s]).wait()
            for t in range(2):
                q = 2 * st + t
                block = arrived[s, q].reshape(ROWS, 128).astype(F32)
                mirror[pl.ds(pl.multiple_of(s * 1152 + q * ROWS, 16), ROWS), :] = block
        return 0

    span = BACK_ROWS * CHUNK
    first = lax.broadcasted_iota(jnp.int32, (span, 128), 1) < 64
    code = lax.rem(lax.broadcasted_iota(jnp.int32, (span, 128), 1), 64).astype(F32)
    first_chunk = lax.broadcasted_iota(jnp.int32, (CHUNK, 128), 1) < 64
    small = lax.broadcasted_iota(jnp.int32, (8, 128), 1) < 64
    sel_row = lax.broadcasted_iota(jnp.int32, (128, 256), 0)
    sel_lane = lax.broadcasted_iota(jnp.int32, (128, 256), 1)
    sel_add = HALF * lax.rem(sel_lane // 64, 2) + sel_lane // 128

    def backward_rows(k, g):
        col_weight = jnp.broadcast_to(goals[k][:, 48:49].astype(F32), (CHUNK, 128))
        parts, weights, aims, own = [], [], [], []
        for n in range(BACK_ROWS):
            p = BACK_ROWS * g + n
            for s in range(4):
                at = s * 1152 + k * (8 * ROWS) + (p // 8) * 16 + lax.rem(p, 8)
                x0 = mirror[pl.ds(at, 8, stride=ROWS), :]
                x1 = mirror[pl.ds(at + 8, 8, stride=ROWS), :]
                parts.append(jnp.where(small, x0, pltpu.roll(x1, 64, axis=1)))
                parts.append(jnp.where(small, pltpu.roll(x0, 64, axis=1), x1))
            m0 = mask[r * ROWS + p].astype(F32)
            m1 = mask[r * ROWS + p + HALF].astype(F32)
            weights.append(col_weight * jnp.where(first_chunk, m0, m1))
            own += [logits[p // 2, a, n % 2, k].astype(F32) for a in range(4)]
            if n % 2 == 0:
                both = dot(goals[k], (sel_row == sel_add + p).astype(BF16))
                aims += [both[:, :128], both[:, 128:]]
        scores = jnp.concatenate(own, axis=0) + jnp.concatenate(parts, axis=0)
        low_max = jnp.max(jnp.where(first, scores, -jnp.inf), axis=-1, keepdims=True)
        high_max = jnp.max(jnp.where(first, -jnp.inf, scores), axis=-1, keepdims=True)
        expo = jnp.exp(scores - jnp.where(first, low_max, high_max))
        low_sum = jnp.sum(jnp.where(first, expo, 0.0), axis=-1, keepdims=True)
        high_sum = jnp.sum(jnp.where(first, 0.0, expo), axis=-1, keepdims=True)
        prob = expo * jnp.where(first, 1.0 / low_sum, 1.0 / high_sum)
        aim = jnp.concatenate(aims, axis=0)
        dlog = ((prob - jnp.where(aim == code, 1.0, 0.0)) * jnp.concatenate(weights, axis=0)).astype(BF16)
        dfin = dot(dlog, bins2_t[...])
        ids = [BACK_ROWS * g + n + HALF * h for h in range(2) for n in range(BACK_ROWS)]
        grad = jnp.concatenate([dfin[:, :128], dfin[:, 128:]], axis=0)
        slopes = jnp.concatenate([slope[i, k] for i in ids], axis=0)
        dh = (dot(grad.astype(BF16), half_shrink_t[...]) * slopes.astype(F32)).astype(BF16)
        dxn = dot(dh, expand_t[...])
        mid = jnp.concatenate([middle[i, k] for i in ids], axis=0)
        xhat, scale = normalize(mid.astype(F32))
        overlap = jnp.mean(dxn * xhat, axis=-1, keepdims=True)
        res = (grad + scale * (dxn - xhat * overlap)).astype(BF16)
        for n, i in enumerate(ids):
            grads[k, i] = res[n * CHUNK : (n + 1) * CHUNK]

    def backward_chunk(k, _):
        lax.fori_loop(4 * k, 4 * k + 4, take_mirror, 0)

        def backward_step(g, _):
            backward_rows(k, g)
            return 0

        lax.fori_loop(0, HALF // BACK_ROWS, backward_step, 0, unroll=BACK_UNROLL)
        pltpu.make_async_copy(grads.at[k], out_hbm.at[k], out_sem.at[k]).start()
        return 0

    lax.fori_loop(0, 3, backward_chunk, 0)

    for k in range(3):
        pltpu.make_async_copy(grads.at[k], out_hbm.at[k], out_sem.at[k]).wait()

    def drain_right(k, _):
        right_copy(r, k, partner).wait_send()
        return 0

    lax.fori_loop(0, 31, drain_right, 0)

    def drain_left(k, _):
        @pl.when(jnp.logical_not(left_self(k)))
        def _():
            left_copy(k).wait_send()

        return 0

    lax.fori_loop(0, 32, drain_left, 0)

    def drain_mirror(st, _):
        @pl.when(is_relayed(st))
        def _():
            relay_copy(st).wait_send()

        @pl.when(jnp.logical_not(is_relayed(st)))
        def _():
            for a in range(4):
                @pl.when(jnp.logical_not(mirror_is_self(a)))
                def _():
                    mirror_copy(st, a).wait_send()

        return 0

    lax.fori_loop(0, 12, drain_mirror, 0)

    def drain_pass(st, _):
        @pl.when(jnp.logical_and(diagonal, goes_round(st)))
        def _():
            for k in range(1, 4):
                for a in range(4):
                    pass_copy(lax.rem(y + k, 4), st, a).wait_send()

        return 0

    lax.fori_loop(0, 12, drain_pass, 0)


def unpermute(grads, out):
    for i in range(out.shape[0]):
        rows = jnp.concatenate([grads[k, i].astype(F32) for k in range(3)], axis=0)
        out[i] = permute(rows, BACK_ORDER).astype(BF16)


def per_device(
    alignment, pair_act, targets, crop_mask, projection_weight, w_outer, w_expand, w_shrink, w_bins
):
    vmem = pl.BlockSpec(memory_space=pltpu.VMEM)
    anywhere = pl.BlockSpec(memory_space=pl.ANY)
    grads = pl.pallas_call(
        kernel,
        out_shape=jax.ShapeDtypeStruct((3, ROWS, CHUNK, CH), BF16),
        in_specs=[vmem, anywhere, vmem, vmem] + [pl.BlockSpec(memory_space=pltpu.SMEM)] + [vmem] * 5,
        out_specs=anywhere,
        scratch_shapes=[
            pltpu.VMEM((32, 96, 128), BF16),
            pltpu.VMEM((32, 32, 128), BF16),
            pltpu.VMEM((4, 32, 128), BF16),
            pltpu.VMEM((3072 + 96, 128), F32),
            pltpu.VMEM((1024 + 32, 128), F32),
            pltpu.VMEM((768, 128), BF16),
            pltpu.VMEM((16, 3, 128, 256), BF16),
            pltpu.VMEM((12, 1024, 768), BF16),
            pltpu.VMEM((ROWS, 3, CHUNK, CH), BF16),
            pltpu.VMEM((ROWS, 3, CHUNK, HID), BF16),
            pltpu.VMEM((12, 4, 2, 3, 16, 128), BF16),
            pltpu.VMEM((4, HALF, 3, 16, 128), BF16),
            pltpu.VMEM((4 * HALF * ROWS + ROWS, 128), F32),
            pltpu.VMEM((4, 12, 4, 2, 3, 16, 128), BF16),
            pltpu.VMEM((128, 1024), BF16),
            pltpu.VMEM((128, HID), BF16),
            pltpu.VMEM((256, 128), BF16),
            pltpu.VMEM((128, HID), BF16),
            pltpu.VMEM((HID, 128), BF16),
            pltpu.VMEM((128, 256), BF16),
            pltpu.VMEM((3, CHUNK, 128), BF16),
            pltpu.VMEM((6, 128, 128), F32),
            pltpu.VMEM((6, 128, 128), F32),
            pltpu.VMEM((ROWS, COLS, CH), BF16),
            pltpu.VMEM((3, ROWS, CHUNK, CH), BF16),
            pltpu.SemaphoreType.DMA(()),
            pltpu.SemaphoreType.DMA((3,)),
            pltpu.SemaphoreType.DMA((31,)),
            pltpu.SemaphoreType.DMA((32,)),
            pltpu.SemaphoreType.DMA((32,)),
            pltpu.SemaphoreType.DMA((32,)),
            pltpu.SemaphoreType.DMA((12, 4)),
            pltpu.SemaphoreType.DMA((12, 4)),
            pltpu.SemaphoreType.DMA((12,)),
            pltpu.SemaphoreType.DMA((4, 12)),
            pltpu.SemaphoreType.DMA((4, 12, 4)),
        ],
        compiler_params=pltpu.CompilerParams(
            collective_id=0, has_side_effects=True, vmem_limit_bytes=63 * 1024 * 1024
        ),
    )(
        alignment, pair_act, targets, crop_mask.reshape(12, 128), crop_mask, projection_weight.T,
        w_outer, w_expand, w_shrink, w_bins.T,
    )
    return pl.pallas_call(
        unpermute,
        grid=(ROWS // EMIT_ROWS,),
        out_shape=jax.ShapeDtypeStruct((ROWS, COLS, CH), BF16),
        in_specs=[pl.BlockSpec((3, EMIT_ROWS, CHUNK, CH), lambda i: (0, i, 0, 0))],
        out_specs=pl.BlockSpec((EMIT_ROWS, COLS, CH), lambda i: (i, 0, 0)),
    )(grads)


def solution(mesh):
    in_specs = (
        P("row", "col", None), P("row", "col", None), P("row", "col"),
        P(), P(), P(), P(), P(), P(),
    )
    return jax.shard_map(
        per_device, mesh=mesh, in_specs=in_specs, out_specs=P("row", "col", None), check_vma=False
    )
```
